32 devices in a mesh: section: 4 (over x, core), col: 4 (over z), row: 2 (over y).
Axes of the slice: x: 2, y: 2, z: 4, core: 2. Of those that a mesh axis runs over, the one named last changes fastest.
Arguments:
- features: bfloat16 [4, 32, 128, 256], P(None, 'row', 'col'), may hold values from -6 to 6
- conv_weight: bfloat16 [4, 3, 3, 256, 256], P('section'), may hold values from -0.125 to 0.125
- tissue: int32 [4, 32, 128], P(None, 'row', 'col'), may hold values 0 or 1
Outputs:
- section_out: bfloat16 [4, 4, 32, 128, 256], P('section', None, 'row', 'col')
- loss_map: float32 [4, 4, 32, 128], P('section', None, 'row', 'col')
The draws below stay inside these ranges and needn't reach their ends.
All inputs are finite; a program needn't handle non-finite values. No bound on the sum of `tissue` on one device may be relied on, other than what follows from the above.
Results may differ from the reference program's by a relative error of at most 0.008.
Values may be sent and summed in bfloat16 or wider, within the bound.
A program may use at most 64 MiB of HBM per device.

```python
import jax
import jax.numpy as jnp
from jax import lax

C = 256
DILATION_RATE = 2
MICRO = 4
LAYERS = 4
H = 32
W = 128


def place_ends(values, rng, least, high):
    extent = values.shape
    place = [jax.random.randint(jax.random.fold_in(rng, axis), (), 0, extent[axis]) for axis in range(len(extent))]
    values = values.at[tuple(place)].set(least)
    longest = extent.index(max(extent))
    place[longest] = (place[longest] + 1) % extent[longest]
    return values.at[tuple(place)].set(high)


def levels(stream_key, dims, cuts, smallest, top_value):
    factor_of = 1.0
    for position, shards_of in cuts:
        heights = jax.random.uniform(jax.random.fold_in(jax.random.fold_in(stream_key, 6), position), (shards_of,), jnp.float32, smallest / len(cuts), top_value / len(cuts))
        factor_of = factor_of * jnp.repeat(jnp.exp(heights), dims[position] // shards_of).reshape((-1,) + (1,) * (len(dims) - 1 - position))
    return factor_of


def bell_draw(own_key, dims, spread, reach, pieces=(), dtype=jnp.bfloat16):
    values = jax.random.normal(own_key, dims, jnp.float32) * spread
    if len(pieces) > 0:
        values = levels(own_key, dims, pieces, -0.22, 0.18) * values
    return jnp.clip(values, min=-reach, max=reach).astype(dtype)


def setup_inputs(seed: int = 0) -> dict:
    arg_keys = jax.random.split(jax.random.key(seed), 4)
    features = bell_draw(arg_keys[0], (MICRO, H, W, C), 1.0, 6.0, ((1, 2), (2, 4)))
    conv_weight = bell_draw(arg_keys[1], (LAYERS, 3, 3, C, C), (9 * C) ** -0.5, 0.125, ((0, 4),))
    tissue = place_ends((jax.random.randint(arg_keys[2], (MICRO, H, W), 0, 2) < 1).astype(jnp.int32), jax.random.fold_in(arg_keys[2], 1), 0, 1)
    return {"features": features, "conv_weight": conv_weight, "tissue": tissue}


residual_scale = 0.8


def apply_layer(current_activation, filter_weight):
    hidden_features = lax.conv_general_dilated(current_activation.astype(jnp.float32), filter_weight.astype(jnp.float32), (1, 1), ((DILATION_RATE, DILATION_RATE), (DILATION_RATE, DILATION_RATE)), rhs_dilation=(DILATION_RATE, DILATION_RATE), dimension_numbers=("NHWC", "HWIO", "NHWC"), precision=lax.Precision.HIGHEST)
    return (residual_scale * (current_activation.astype(jnp.float32) + jnp.maximum(hidden_features, 0.0))).astype(jnp.bfloat16)


def reference(features, conv_weight, tissue):
    flipped = features[:, :, ::-1, :]
    current_activation = jnp.stack([features, flipped], 1).reshape(MICRO * 2, H, W, C)
    stacked_out = []
    losses = []
    mask_float = tissue.astype(jnp.float32)
    for layer_index in range(LAYERS):
        current_activation = apply_layer(current_activation, conv_weight[layer_index])
        split_pairs = current_activation.reshape(MICRO, 2, H, W, C)
        primary = split_pairs[:, 0]
        restored = split_pairs[:, 1][:, :, ::-1, :]
        deviation = primary.astype(jnp.float32) - restored.astype(jnp.float32)
        losses.append(mask_float * jnp.mean(deviation * deviation, -1))
        stacked_out.append(primary)
    return jnp.stack(stacked_out), jnp.stack(losses)
```

```python
import functools

import jax
import jax.numpy as jnp
from jax import lax
from jax.experimental import pallas as pl
from jax.experimental.pallas import tpu as pltpu
from jax.sharding import PartitionSpec as P

DILATION_RATE = 2
TAPS = 3
ORDER = (1, 0, 2)
residual_scale = 0.8
MESH = pl.DeviceIdType.MESH
OWN, DIRECT, ROW, COL, DIAG, SIB = range(6)


def kernel(cfg, f_ref, w_ref, out_ref, loss_ref, fwin, wall, a0, a1, b0, b1, s0, s1, stage, lstage,
           hs_sem, hr_sem, ws_sem, wr_sem, ks_sem, kr_sem, go_sem, os_sem, or_sem, ls_sem, lr_sem, loc_sem):
    S, M, R, CL, C, n_col, halo, hb, NR, NC = cfg
    me = lax.axis_index("section")
    col = lax.axis_index("col")
    row = lax.axis_index("row")
    micro = lax.rem(me, M)
    group = S // M
    replica = me // M
    low = lax.rem(me, 2)
    sib = me + 1 - 2 * low
    pairs = S // 2
    my_pair = me // 2
    other_row = 1 - row
    mate = col + 1 - 2 * lax.rem(col, 2)
    has_left = col > 0
    has_right = col < n_col - 1
    quarter = C // 4
    direct = quarter // 2
    my_q = 2 * row + lax.rem(col, 2)

    def at(section=None, c=None, r=None):
        return {
            "section": me if section is None else section,
            "col": col if c is None else c,
            "row": row if r is None else r,
        }

    barrier = pltpu.get_barrier_semaphore()

    def hello(dev):
        pl.semaphore_signal(barrier, inc=1, device_id=dev, device_id_type=MESH)

    for d in range(1, S):
        hello(at(section=lax.rem(me + d, S)))
    hello(at(r=other_row))

    @pl.when(has_left)
    def _():
        hello(at(c=col - 1))
        hello(at(c=col - 1, r=other_row))

    @pl.when(has_right)
    def _():
        hello(at(c=col + 1))
        hello(at(c=col + 1, r=other_row))

    own_w = [pltpu.make_async_copy(w_ref.at[:, kx], wall.at[me, kx], loc_sem.at[kx]) for kx in range(TAPS)]
    own_f = pltpu.make_async_copy(
        f_ref.at[micro],
        fwin.at[pl.ds(row * halo, R), pl.ds(hb, CL)],
        loc_sem.at[3],
    )
    own_f.start()
    for kx in ORDER:
        own_w[kx].start()

    zeros = jnp.zeros((DILATION_RATE * NC, C), jnp.bfloat16)
    for ref in (a0, b0, b1, a1):
        ref[0 : DILATION_RATE * NC, :] = zeros
        ref[(DILATION_RATE + NR) * NC :, :] = zeros

    greeted = 1 + (S - 1) + 2 * has_left.astype(jnp.int32) + 2 * has_right.astype(jnp.int32)
    pl.semaphore_wait(barrier, greeted)

    def remote(src, dst, s_sem, r_sem, dev):
        return pltpu.make_async_remote_copy(
            src_ref=src, dst_ref=dst, send_sem=s_sem, recv_sem=r_sem,
            device_id=dev, device_id_type=MESH,
        )

    def twin(k):
        a, b, res, bit = my_pair, k, 0, 1
        while bit < pairs:
            res = res + bit * lax.rem(a // bit + b // bit, 2)
            bit *= 2
        return 2 * res + low

    def rows_of(kind):
        if kind == OWN:
            return my_q * quarter, quarter
        if kind == DIRECT:
            return (3 - my_q) * quarter, direct
        if kind == ROW:
            return (my_q + 2 - 4 * row) * quarter, quarter
        if kind == COL:
            return (my_q + 1 - 2 * lax.rem(col, 2)) * quarter, quarter
        if kind == DIAG:
            return (3 - my_q) * quarter + direct, quarter - direct

    def part(kind):
        start, size = rows_of(kind)
        return pl.ds(pl.multiple_of(start, 16), size)

    def sent_part(kind):
        if kind == DIAG:
            return pl.ds(pl.multiple_of(my_q * quarter + direct, 16), quarter - direct)
        return part(OWN)

    def give(k, kx, kind):
        piece = part(kind)
        return remote(w_ref.at[:, kx, piece], wall.at[me, kx, :, piece],
                      ws_sem.at[k, kx, kind], wr_sem.at[k, kx, kind], at(section=twin(k)))

    def forward(l, k, kx, kind):
        piece = sent_part(kind)
        dev = {ROW: at(r=other_row), COL: at(c=mate), DIAG: at(c=mate, r=other_row)}[kind]
        slot = wall.at[l, kx, :, piece]
        return remote(slot, slot, ws_sem.at[k, kx, kind], wr_sem.at[k, kx, kind], dev)

    def arrival(l, k, kx, kind):
        slot = wall.at[l, kx, :, part(kind)]
        return remote(slot, slot, ws_sem.at[k, kx, kind], wr_sem.at[k, kx, kind], at(section=twin(k)))

    def share(l, k, kx):
        slot = wall.at[l, kx]
        return remote(slot, slot, ws_sem.at[k, kx, SIB], wr_sem.at[k, kx, SIB], at(section=sib))

    def to_sib(kx):
        return remote(w_ref.at[:, kx], wall.at[me, kx], ks_sem.at[kx], kr_sem.at[kx], at(section=sib))

    def send_own():
        for kx in ORDER:
            for k in range(1, pairs):
                give(k, kx, OWN).start()
                give(k, kx, DIRECT).start()

    def own_sent():
        for kx in ORDER:
            for k in range(1, pairs):
                give(k, kx, OWN).wait_send()
                give(k, kx, DIRECT).wait_send()

    def relay(l, kx):
        for k in range(1, pairs):
            @pl.when(twin(k) == l)
            def _(k=k):
                arrival(l, k, kx, OWN).wait_recv()
                forward(l, k, kx, ROW).start()
                forward(l, k, kx, COL).start()
                forward(l, k, kx, DIAG).start()

    def gather(l, kx):
        for k in range(1, pairs):
            @pl.when(twin(k) == l)
            def _(k=k):
                for kind in (DIRECT, ROW, COL, DIAG):
                    arrival(l, k, kx, kind).wait_recv()
                share(l, k, kx).start()

    def complete(l, kx, gathered):
        @pl.when(me == l)
        def _():
            own_w[kx].wait()

        @pl.when(sib == l)
        def _():
            to_sib(kx).wait_recv()

        if gathered is None:
            gather(l, kx)
        elif gathered is not True:
            pl.when(jnp.logical_not(gathered))(lambda: gather(l, kx))
        for k in range(1, pairs):
            @pl.when(twin(k) + 1 - 2 * low == l)
            def _(k=k):
                share(l, k, kx).wait_recv()

    pl.when(low == 0)(send_own)

    rows_here = pl.ds(row * halo, R)
    rows_out = pl.ds((1 - row) * (R - halo), halo)
    rows_in = pl.ds(row * R, halo)
    mid = pl.ds(hb, CL)
    lcols, rcols = pl.ds(0, hb), pl.ds(hb + CL, hb)
    first, last = pl.ds(0, hb), pl.ds(CL - hb, hb)
    mine = f_ref.at[micro]
    to_left = remote(mine.at[:, first], fwin.at[rows_here, rcols], hs_sem.at[0], hr_sem.at[0], at(c=col - 1))
    to_right = remote(mine.at[:, last], fwin.at[rows_here, lcols], hs_sem.at[1], hr_sem.at[1], at(c=col + 1))
    to_row = remote(mine.at[rows_out], fwin.at[rows_in, mid], hs_sem.at[2], hr_sem.at[2], at(r=other_row))
    to_dl = remote(mine.at[rows_out, first], fwin.at[rows_in, rcols], hs_sem.at[3], hr_sem.at[3], at(c=col - 1, r=other_row))
    to_dr = remote(mine.at[rows_out, last], fwin.at[rows_in, lcols], hs_sem.at[4], hr_sem.at[4], at(c=col + 1, r=other_row))
    to_row.start()

    @pl.when(has_left)
    def _():
        to_left.start()
        to_dl.start()

    @pl.when(has_right)
    def _():
        to_right.start()
        to_dr.start()

    for kx in ORDER:
        to_sib(kx).start()

    def first_even(j):
        kx = ORDER[j]
        relay(0, kx)
        if pairs > 1:
            pl.when(my_pair == 0)(lambda: relay(2, kx))

    first_even(0)

    @pl.when(low == 0)
    def _():
        own_sent()
        pl.semaphore_signal(go_sem, inc=1, device_id=at(section=sib), device_id_type=MESH)

    @pl.when(low == 1)
    def _():
        pl.semaphore_wait(go_sem, 1)
        send_own()

    first_even(1)
    first_even(2)

    own_f.wait()
    to_row.wait()

    @pl.when(has_left)
    def _():
        to_left.wait_send()
        to_dl.wait_send()
        to_right.wait_recv()
        to_dr.wait_recv()

    @pl.when(has_right)
    def _():
        to_right.wait_send()
        to_dr.wait_send()
        to_left.wait_recv()
        to_dl.wait_recv()

    def in_map_only(v):
        return jnp.concatenate(
            [
                jnp.where(has_left, v[:, :halo], 0.0),
                v[:, halo : halo + CL],
                jnp.where(has_right, v[:, halo + CL :], 0.0),
            ],
            axis=1,
        )

    off = hb - halo
    for i in range(0, NR, 4):
        v = fwin[i : i + 4].astype(jnp.float32)[:, off : off + NC, :]
        v = in_map_only(v).astype(jnp.bfloat16)
        a0[(i + DILATION_RATE) * NC : (i + 4 + DILATION_RATE) * NC, :] = v.reshape(4 * NC, C)

    def after(l, j):
        kx = ORDER[j]
        if l == 0:
            pl.when(my_pair > 0)(lambda: relay(1, kx))
        if pairs > 1:
            if l == 0 and j == 2:
                def early():
                    gather(2, ORDER[0])
                    gather(2, ORDER[1])
                pl.when(my_pair == 0)(early)
            if l == 1 and j == 0:
                pl.when(my_pair == 0)(lambda: relay(3, ORDER[0]))
            if l == 1 and j == 1:
                def late():
                    gather(2, ORDER[2])
                    relay(3, ORDER[1])
                pl.when(my_pair == 0)(late)
            if l == 2 and j == 0:
                pl.when(my_pair == 0)(lambda: relay(3, ORDER[2]))
        if j == 2 and l + 2 < S and l + 2 >= 2:
            t = l + 2
            for kk in ORDER:
                if t in (2, 3):
                    pl.when(my_pair > 0)(lambda t=t, kk=kk: relay(t, kk))
                else:
                    relay(t, kk)

    def out_copy(l, h):
        n = NR - DILATION_RATE * (l + 1)
        half = R // 2
        place = pl.ds(pl.multiple_of((row if h == 0 else other_row) * half, half), half)
        src = stage.at[l, pl.ds(row * (n - R) + (row if h == 0 else other_row) * half, half)]
        return src, out_ref.at[micro, place]

    def loss_copy(l):
        n = NR - DILATION_RATE * (l + 1)
        return lstage.at[l, pl.ds(row * (n - R), R)], loss_ref.at[micro]

    def out_send(l, h):
        src, dst = out_copy(l, h)
        return remote(src, dst, os_sem.at[l, h], or_sem.at[micro, h], at(section=l))

    def loss_send(l):
        src, dst = loss_copy(l)
        return remote(src, dst, ls_sem.at[l], lr_sem.at[micro], at(section=l))

    def out_keep(l, h):
        src, dst = out_copy(l, h)
        return pltpu.make_async_copy(src, dst, loc_sem.at[4 + h])

    def loss_keep(l):
        src, dst = loss_copy(l)
        return pltpu.make_async_copy(src, dst, loc_sem.at[6])

    def sends(l):
        return jnp.logical_and(replica == l % group, me != l)

    def keeps(l):
        return jnp.logical_and(replica == l % group, me == l)

    eye = lax.broadcasted_iota(jnp.int32, (1, CL, 128), 1) == lax.broadcasted_iota(jnp.int32, (1, CL, 128), 2)

    for l in range(S):
        n = NR - DILATION_RATE * (l + 1)
        r0 = row * (NR - n)
        chunk = n // 2
        m = chunk * NC
        cur, nxt = ((a0, a1), (b0, b1))[l % 2], ((a0, a1), (b0, b1))[(l + 1) % 2]
        sums = (s0, s1)
        shared = l == 0
        for j, kx in enumerate(ORDER):
            complete(l, kx, (my_pair == 0) if l == 2 else None)
            w = wall[l, kx].reshape(TAPS * C, C)
            for q in range(2):
                place = row if q == 0 else other_row
                base = r0 + place * chunk
                keep = pl.ds(q * m, m)
                centre = pl.ds(pl.multiple_of((base + DILATION_RATE) * NC, 16), m)
                products = []
                for mem in range(1 if shared else 2):
                    lhs = jnp.concatenate(
                        [cur[mem][pl.ds(pl.multiple_of((base + DILATION_RATE * ky) * NC, 16), m), :] for ky in range(TAPS)],
                        axis=1,
                    )
                    products.append(jnp.dot(lhs, w, preferred_element_type=jnp.float32))
                if shared:
                    products.append(products[0])
                if kx == 1:
                    for mem in range(1 if shared else 2):
                        sums[mem][keep, :] = products[mem]
                    continue
                shift = DILATION_RATE if kx == 0 else m - DILATION_RATE
                moved = [pltpu.roll(products[mem], shift if mem == 0 else m - shift, 0) for mem in range(2)]
                if kx == 0:
                    before = [sums[0 if shared else mem][keep, :] for mem in range(2)]
                    for mem in range(2):
                        sums[mem][keep, :] = before[mem] + moved[mem]
                    continue
                ys = []
                for mem in range(2):
                    conv = sums[mem][keep, :] + moved[mem]
                    res = cur[0 if shared else mem][centre, :].astype(jnp.float32)
                    y = residual_scale * (res + jnp.maximum(conv, 0.0))
                    y = in_map_only(y.reshape(chunk, NC, C)).astype(jnp.bfloat16)
                    if l < S - 1:
                        nxt[mem][centre, :] = y.reshape(m, C)
                    ys.append(y.astype(jnp.float32)[:, halo : halo + CL, :])
                stage[l, pl.ds(place * chunk, chunk)] = ys[0].astype(jnp.bfloat16)
                d = ys[0] - ys[1]
                d = jnp.sum(d * d, axis=-1, keepdims=True)
                lstage[l, pl.ds(place * chunk, chunk)] = jnp.sum(jnp.where(eye, d, 0.0), axis=1, keepdims=True)

                @pl.when(sends(l))
                def _(l=l, q=q):
                    out_send(l, q).start()
                    if q == 1:
                        loss_send(l).start()

                @pl.when(keeps(l))
                def _(l=l, q=q):
                    out_keep(l, q).start()
                    if q == 1:
                        loss_keep(l).start()
            after(l, j)

    @pl.when(low == 1)
    def _():
        own_sent()

    for k in range(1, pairs):
        for kx in ORDER:
            for kind in (ROW, COL, DIAG):
                forward(twin(k), k, kx, kind).wait_send()
            share(twin(k), k, kx).wait_send()
    for kx in ORDER:
        to_sib(kx).wait_send()

    for l in range(S):
        @pl.when(sends(l))
        def _(l=l):
            out_send(l, 0).wait_send()
            out_send(l, 1).wait_send()
            loss_send(l).wait_send()

        @pl.when(keeps(l))
        def _(l=l):
            out_keep(l, 0).wait()
            out_keep(l, 1).wait()
            loss_keep(l).wait()

    for b in range(M):
        sender = b + M * lax.rem(me, group)

        @pl.when(sender != me)
        def _(b=b, sender=sender):
            for h in range(2):
                half = R // 2
                place = pl.ds(pl.multiple_of((row if h == 0 else other_row) * half, half), half)
                dst = out_ref.at[b, place]
                remote(dst, dst, os_sem.at[0, h], or_sem.at[b, h], at(section=sender)).wait_recv()
            remote(loss_ref.at[b], loss_ref.at[b], ls_sem.at[0], lr_sem.at[b], at(section=sender)).wait_recv()


def local(features, conv_weight, tissue):
    S = lax.axis_size("section")
    n_col = lax.axis_size("col")
    M, R, CL, C = features.shape
    halo = DILATION_RATE * S
    hb = -(-halo // 16) * 16
    NR, NC = R + halo, CL + 2 * halo
    pairs = S // 2
    rows_max = (NR - DILATION_RATE) * NC
    cfg = (S, M, R, CL, C, n_col, halo, hb, NR, NC)
    anyspec = pl.BlockSpec(memory_space=pl.ANY)
    dma = pltpu.SemaphoreType.DMA
    act = pltpu.VMEM(((NR + 2 * DILATION_RATE) * NC, C), jnp.bfloat16)
    out, sums = pl.pallas_call(
        functools.partial(kernel, cfg),
        out_shape=(
            jax.ShapeDtypeStruct((M, R, CL, C), jnp.bfloat16),
            jax.ShapeDtypeStruct((M, R, 1, 128), jnp.float32),
        ),
        in_specs=[anyspec, anyspec],
        out_specs=(anyspec, anyspec),
        scratch_shapes=[
            pltpu.VMEM((NR, CL + 2 * hb, C), jnp.bfloat16),
            pltpu.VMEM((S, TAPS, TAPS, C, C), jnp.bfloat16),
            act, act, act, act,
            pltpu.VMEM((rows_max, C), jnp.float32),
            pltpu.VMEM((rows_max, C), jnp.float32),
            pltpu.VMEM((S, NR, CL, C), jnp.bfloat16),
            pltpu.VMEM((S, NR, 1, 128), jnp.float32),
            dma((5,)), dma((5,)),
            dma((pairs, TAPS, 6)), dma((pairs, TAPS, 6)),
            dma((TAPS,)), dma((TAPS,)),
            pltpu.SemaphoreType.REGULAR,
            dma((S, 2)), dma((M, 2)),
            dma((S,)), dma((M,)),
            dma((7,)),
        ],
        compiler_params=pltpu.CompilerParams(
            collective_id=0, has_side_effects=True, vmem_limit_bytes=60 * 1024 * 1024
        ),
    )(features, conv_weight.reshape(TAPS, TAPS, C, C))
    loss = tissue.astype(jnp.float32) * (sums[:, :, 0, :CL] * (1.0 / C))
    return out[None], loss[None]


def solution(mesh):
    return jax.shard_map(
        local,
        mesh=mesh,
        in_specs=(
            P(None, "row", "col", None),
            P("section", None, None, None, None),
            P(None, "row", "col"),
        ),
        out_specs=(P("section", None, "row", "col", None), P("section", None, "row", "col")),
        check_vma=False,
    )
```

```python
import functools

import jax
import jax.numpy as jnp
from jax import lax
from jax.experimental import pallas as pl
from jax.experimental.pallas import tpu as pltpu
from jax.sharding import PartitionSpec as P

DILATION_RATE = 2
TAPS = 3
ORDER = (1, 0, 2)
residual_scale = 0.8
DIRECT_ROWS = 32
MESH = pl.DeviceIdType.MESH
OWN, DIRECT, ROW, COL, DIAG = range(5)


def kernel(cfg, f_ref, w_ref, out_ref, loss_ref, fwin, lstrip, rstrip, lpack, rpack, wall, a0, a1, b0, b1, s0, s1, stage, lstage,
           hs_sem, hr_sem, ws_sem, wr_sem, ks_sem, kr_sem, go_sem, os_sem, or_sem, ls_sem, lr_sem, loc_sem):
    S, M, R, CL, C, n_col, halo, NR, NC = cfg
    me = lax.axis_index("section")
    col = lax.axis_index("col")
    row = lax.axis_index("row")
    micro = lax.rem(me, M)
    group = S // M
    replica = me // M
    low = lax.rem(me, 2)
    sib = me + 1 - 2 * low
    pairs = S // 2
    my_pair = me // 2
    other_row = 1 - row
    mate = col + 1 - 2 * lax.rem(col, 2)
    has_left = col > 0
    has_right = col < n_col - 1
    quarter = C // 4
    direct = DIRECT_ROWS * quarter // 64
    my_q = 2 * row + lax.rem(col, 2)

    def at(section=None, c=None, r=None):
        return {
            "section": me if section is None else section,
            "col": col if c is None else c,
            "row": row if r is None else r,
        }

    barrier = pltpu.get_barrier_semaphore()

    def hello(dev):
        pl.semaphore_signal(barrier, inc=1, device_id=dev, device_id_type=MESH)

    for d in range(1, S):
        hello(at(section=lax.rem(me + d, S)))
    hello(at(r=other_row))

    @pl.when(has_left)
    def _():
        hello(at(c=col - 1))
        hello(at(c=col - 1, r=other_row))

    @pl.when(has_right)
    def _():
        hello(at(c=col + 1))
        hello(at(c=col + 1, r=other_row))

    own_w = [pltpu.make_async_copy(w_ref.at[:, kx], wall.at[me, kx], loc_sem.at[kx]) for kx in range(TAPS)]
    own_f = pltpu.make_async_copy(
        f_ref.at[micro],
        fwin.at[pl.ds(row * halo, R)],
        loc_sem.at[3],
    )
    own_f.start()
    for kx in ORDER:
        own_w[kx].start()

    zeros = jnp.zeros((DILATION_RATE * NC, C), jnp.bfloat16)
    for ref in (a0, b0, b1, a1):
        ref[0 : DILATION_RATE * NC, :] = zeros
        ref[(DILATION_RATE + NR) * NC :, :] = zeros

    own_f.wait()
    edge = fwin[pl.ds(row * halo, R)].astype(jnp.float32)
    lpack[...] = edge[:, :halo, :].reshape(R * halo, C).astype(jnp.bfloat16)
    rpack[...] = edge[:, CL - halo :, :].reshape(R * halo, C).astype(jnp.bfloat16)

    greeted = 1 + (S - 1) + 2 * has_left.astype(jnp.int32) + 2 * has_right.astype(jnp.int32)
    pl.semaphore_wait(barrier, greeted)

    def remote(src, dst, s_sem, r_sem, dev):
        return pltpu.make_async_remote_copy(
            src_ref=src, dst_ref=dst, send_sem=s_sem, recv_sem=r_sem,
            device_id=dev, device_id_type=MESH,
        )

    def twin(k):
        a, b, res, bit = my_pair, k, 0, 1
        while bit < pairs:
            res = res + bit * lax.rem(a // bit + b // bit, 2)
            bit *= 2
        return 2 * res + low

    def rows_of(kind):
        if kind == OWN:
            return my_q * quarter, quarter
        if kind == DIRECT:
            return (3 - my_q) * quarter, direct
        if kind == ROW:
            return (my_q + 2 - 4 * row) * quarter, quarter
        if kind == COL:
            return (my_q + 1 - 2 * lax.rem(col, 2)) * quarter, quarter
        if kind == DIAG:
            return (3 - my_q) * quarter + direct, quarter - direct

    routed = (ROW, COL, DIAG) if direct < quarter else (ROW, COL)

    def part(kind):
        start, size = rows_of(kind)
        return pl.ds(pl.multiple_of(start, 16), size)

    def sent_part(kind):
        if kind == DIAG:
            return pl.ds(pl.multiple_of(my_q * quarter + direct, 16), quarter - direct)
        return part(OWN)

    def give(k, kx, kind):
        piece = part(kind)
        return remote(w_ref.at[:, kx, piece], wall.at[me, kx, :, piece],
                      ws_sem.at[k, kx, kind], wr_sem.at[k, kx, kind], at(section=twin(k)))

    def forward(l, k, kx, kind):
        piece = sent_part(kind)
        dev = {ROW: at(r=other_row), COL: at(c=mate), DIAG: at(c=mate, r=other_row)}[kind]
        slot = wall.at[l, kx, :, piece]
        return remote(slot, slot, ws_sem.at[k, kx, kind], wr_sem.at[k, kx, kind], dev)

    def arrival(l, k, kx, kind):
        slot = wall.at[l, kx, :, part(kind)]
        return remote(slot, slot, ws_sem.at[k, kx, kind], wr_sem.at[k, kx, kind], at(section=twin(k)))

    SHARES = (OWN, ROW, COL, DIAG)

    def share(l, k, kx, kind):
        start = rows_of(DIRECT)[0] if kind == DIAG else rows_of(kind)[0]
        slot = wall.at[l, kx, :, pl.ds(pl.multiple_of(start, 16), quarter)]
        n = 5 + SHARES.index(kind)
        return remote(slot, slot, ws_sem.at[k, kx, n], wr_sem.at[k, kx, n], at(section=sib))

    def to_sib(kx):
        return remote(w_ref.at[:, kx], wall.at[me, kx], ks_sem.at[kx], kr_sem.at[kx], at(section=sib))

    def send_own():
        for kind in (OWN, DIRECT):
            for kx in ORDER:
                for k in range(1, pairs):
                    give(k, kx, kind).start()

    def own_sent(kind):
        for kx in ORDER:
            for k in range(1, pairs):
                give(k, kx, kind).wait_send()

    def relay(l, kx):
        for k in range(1, pairs):
            @pl.when(twin(k) == l)
            def _(k=k):
                arrival(l, k, kx, OWN).wait_recv()
                for kind in routed:
                    forward(l, k, kx, kind).start()
                share(l, k, kx, OWN).start()

    def gather(l, kx):
        for k in range(1, pairs):
            @pl.when(twin(k) == l)
            def _(k=k):
                for kind in (COL, ROW):
                    arrival(l, k, kx, kind).wait_recv()
                    share(l, k, kx, kind).start()
                arrival(l, k, kx, DIRECT).wait_recv()
                if DIAG in routed:
                    arrival(l, k, kx, DIAG).wait_recv()
                share(l, k, kx, DIAG).start()

    def complete(l, kx, gathered):
        @pl.when(me == l)
        def _():
            own_w[kx].wait()

        @pl.when(sib == l)
        def _():
            to_sib(kx).wait_recv()

        if gathered is None:
            gather(l, kx)
        elif gathered is not True:
            pl.when(jnp.logical_not(gathered))(lambda: gather(l, kx))
        for k in range(1, pairs):
            @pl.when(twin(k) + 1 - 2 * low == l)
            def _(k=k):
                for kind in SHARES:
                    share(l, k, kx, kind).wait_recv()

    pl.when(low == 0)(send_own)

    def strip(start, count):
        return pl.ds(pl.multiple_of(start * halo, 16), count * halo)

    out_row, in_row = (1 - row) * (R - halo), row * R
    here, across, into = strip(row * halo, R), strip(out_row, halo), strip(in_row, halo)
    to_left = remote(lpack, rstrip.at[here], hs_sem.at[0], hr_sem.at[0], at(c=col - 1))
    to_right = remote(rpack, lstrip.at[here], hs_sem.at[1], hr_sem.at[1], at(c=col + 1))
    to_row = remote(f_ref.at[micro, pl.ds(out_row, halo)], fwin.at[pl.ds(in_row, halo)], hs_sem.at[2], hr_sem.at[2], at(r=other_row))
    to_dl = remote(lpack.at[across], rstrip.at[into], hs_sem.at[3], hr_sem.at[3], at(c=col - 1, r=other_row))
    to_dr = remote(rpack.at[across], lstrip.at[into], hs_sem.at[4], hr_sem.at[4], at(c=col + 1, r=other_row))
    to_row.start()

    @pl.when(has_left)
    def _():
        to_left.start()
        to_dl.start()

    @pl.when(has_right)
    def _():
        to_right.start()
        to_dr.start()

    for kx in ORDER:
        to_sib(kx).start()

    def first_even(j):
        kx = ORDER[j]
        relay(0, kx)
        if pairs > 1:
            pl.when(my_pair == 0)(lambda: relay(2, kx))

    first_even(0)

    @pl.when(low == 0)
    def _():
        own_sent(OWN)
        pl.semaphore_signal(go_sem, inc=1, device_id=at(section=sib), device_id_type=MESH)

    @pl.when(low == 1)
    def _():
        pl.semaphore_wait(go_sem, 1)
        send_own()

    first_even(1)
    first_even(2)

    def in_map_only(v):
        return jnp.concatenate(
            [
                jnp.where(has_left, v[:, :halo], 0.0),
                v[:, halo : halo + CL],
                jnp.where(has_right, v[:, halo + CL :], 0.0),
            ],
            axis=1,
        )

    def fill(start, count):
        for i in range(0, count, 4):
            at_row = start + i
            side = strip(at_row, 4)
            v = jnp.concatenate(
                [
                    jnp.where(has_left, lstrip[side, :].astype(jnp.float32).reshape(4, halo, C), 0.0),
                    fwin[pl.ds(at_row, 4)].astype(jnp.float32),
                    jnp.where(has_right, rstrip[side, :].astype(jnp.float32).reshape(4, halo, C), 0.0),
                ],
                axis=1,
            )
            place = pl.ds(pl.multiple_of((at_row + DILATION_RATE) * NC, 16), 4 * NC)
            a0[place, :] = v.reshape(4 * NC, C).astype(jnp.bfloat16)

    def sides_in():
        @pl.when(has_left)
        def _():
            to_left.wait_send()
            to_right.wait_recv()

        @pl.when(has_right)
        def _():
            to_right.wait_send()
            to_left.wait_recv()

        fill(row * halo, R)

    def rows_come_in():
        to_row.wait()

        @pl.when(has_left)
        def _():
            to_dl.wait_send()
            to_dr.wait_recv()

        @pl.when(has_right)
        def _():
            to_dr.wait_send()
            to_dl.wait_recv()

        fill((1 - row) * R, halo)

    sides_in()
    split_first = halo + DILATION_RATE <= R
    if not split_first:
        rows_come_in()

    def after(l, j):
        if pairs > 1:
            if l == 0 and j == 2:
                def early():
                    gather(2, ORDER[0])
                    gather(2, ORDER[1])
                pl.when(my_pair == 0)(early)
            if l == 1 and j == 0:
                pl.when(my_pair == 0)(lambda: relay(3, ORDER[0]))
            if l == 1 and j == 1:
                def late():
                    gather(2, ORDER[2])
                    relay(3, ORDER[1])
                pl.when(my_pair == 0)(late)
            if l == 2 and j == 0:
                pl.when(my_pair == 0)(lambda: relay(3, ORDER[2]))
        if j == 2 and l + 2 < S and l + 2 >= 2:
            t = l + 2
            for kk in ORDER:
                if t in (2, 3):
                    pl.when(my_pair > 0)(lambda t=t, kk=kk: relay(t, kk))
                else:
                    relay(t, kk)

    def step_done(l, j, q):
        if l == 0 and q == 0:
            pl.when(my_pair > 0)(lambda: relay(1, ORDER[j]))
        if q == 1:
            after(l, j)

    def out_copy(l, h):
        n = NR - DILATION_RATE * (l + 1)
        half = R // 2
        place = pl.ds(pl.multiple_of((row if h == 0 else other_row) * half, half), half)
        src = stage.at[l, pl.ds(row * (n - R) + (row if h == 0 else other_row) * half, half)]
        return src, out_ref.at[micro, place]

    def loss_copy(l):
        n = NR - DILATION_RATE * (l + 1)
        return lstage.at[l, pl.ds(row * (n - R), R)], loss_ref.at[micro]

    def out_send(l, h):
        src, dst = out_copy(l, h)
        return remote(src, dst, os_sem.at[l, h], or_sem.at[micro, h], at(section=l))

    def loss_send(l):
        src, dst = loss_copy(l)
        return remote(src, dst, ls_sem.at[l], lr_sem.at[micro], at(section=l))

    def out_keep(l, h):
        src, dst = out_copy(l, h)
        return pltpu.make_async_copy(src, dst, loc_sem.at[4 + h])

    def loss_keep(l):
        src, dst = loss_copy(l)
        return pltpu.make_async_copy(src, dst, loc_sem.at[6])

    def sends(l):
        return jnp.logical_and(replica == l % group, me != l)

    def keeps(l):
        return jnp.logical_and(replica == l % group, me == l)

    eye = lax.broadcasted_iota(jnp.int32, (1, CL, 128), 1) == lax.broadcasted_iota(jnp.int32, (1, CL, 128), 2)

    for l in range(S):
        n = NR - DILATION_RATE * (l + 1)
        r0 = row * (NR - n)
        chunk = n // 2
        m = chunk * NC
        cur, nxt = ((a0, a1), (b0, b1))[l % 2], ((a0, a1), (b0, b1))[(l + 1) % 2]
        sums = (s0, s1)
        shared = l == 0
        steps = [(j, q) for q in range(2) for j in range(TAPS)] if shared else [(j, q) for j in range(TAPS) for q in range(2)]
        for j, q in steps:
                kx = ORDER[j]
                if q == 0:
                    complete(l, kx, (my_pair == 0) if l == 2 else None)
                if shared and split_first and (j, q) == (0, 1):
                    rows_come_in()
                w = wall[l, kx].reshape(TAPS * C, C)
                place = row if q == 0 else other_row
                base = r0 + place * chunk
                keep = pl.ds(q * m, m)
                centre = pl.ds(pl.multiple_of((base + DILATION_RATE) * NC, 16), m)
                products = []
                for mem in range(1 if shared else 2):
                    lhs = jnp.concatenate(
                        [cur[mem][pl.ds(pl.multiple_of((base + DILATION_RATE * ky) * NC, 16), m), :] for ky in range(TAPS)],
                        axis=1,
                    )
                    products.append(jnp.dot(lhs, w, preferred_element_type=jnp.float32))
                if shared:
                    products.append(products[0])
                if kx == 1:
                    for mem in range(1 if shared else 2):
                        sums[mem][keep, :] = products[mem]
                    step_done(l, j, q)
                    continue
                shift = DILATION_RATE if kx == 0 else m - DILATION_RATE
                moved = [pltpu.roll(products[mem], shift if mem == 0 else m - shift, 0) for mem in range(2)]
                if kx == 0:
                    before = [sums[0 if shared else mem][keep, :] for mem in range(2)]
                    for mem in range(2):
                        sums[mem][keep, :] = before[mem] + moved[mem]
                    step_done(l, j, q)
                    continue
                ys = []
                for mem in range(2):
                    conv = sums[mem][keep, :] + moved[mem]
                    res = cur[0 if shared else mem][centre, :].astype(jnp.float32)
                    y = residual_scale * (res + jnp.maximum(conv, 0.0))
                    y = in_map_only(y.reshape(chunk, NC, C)).astype(jnp.bfloat16)
                    if l < S - 1:
                        nxt[mem][centre, :] = y.reshape(m, C)
                    ys.append(y.astype(jnp.float32)[:, halo : halo + CL, :])
                stage[l, pl.ds(place * chunk, chunk)] = ys[0].astype(jnp.bfloat16)
                d = ys[0] - ys[1]
                d = jnp.sum(d * d, axis=-1, keepdims=True)
                lstage[l, pl.ds(place * chunk, chunk)] = jnp.sum(jnp.where(eye, d, 0.0), axis=1, keepdims=True)

                @pl.when(sends(l))
                def _(l=l, q=q):
                    out_send(l, q).start()
                    if q == 1:
                        loss_send(l).start()

                @pl.when(keeps(l))
                def _(l=l, q=q):
                    out_keep(l, q).start()
                    if q == 1:
                        loss_keep(l).start()
                step_done(l, j, q)

    own_sent(DIRECT)

    @pl.when(low == 1)
    def _():
        own_sent(OWN)

    for k in range(1, pairs):
        for kx in ORDER:
            for kind in routed:
                forward(twin(k), k, kx, kind).wait_send()
            for kind in SHARES:
                share(twin(k), k, kx, kind).wait_send()
    for kx in ORDER:
        to_sib(kx).wait_send()

    for l in range(S):
        @pl.when(sends(l))
        def _(l=l):
            out_send(l, 0).wait_send()
            out_send(l, 1).wait_send()
            loss_send(l).wait_send()

        @pl.when(keeps(l))
        def _(l=l):
            out_keep(l, 0).wait()
            out_keep(l, 1).wait()
            loss_keep(l).wait()

    for b in range(M):
        sender = b + M * lax.rem(me, group)

        @pl.when(sender != me)
        def _(b=b, sender=sender):
            for h in range(2):
                half = R // 2
                place = pl.ds(pl.multiple_of((row if h == 0 else other_row) * half, half), half)
                dst = out_ref.at[b, place]
                remote(dst, dst, os_sem.at[0, h], or_sem.at[b, h], at(section=sender)).wait_recv()
            remote(loss_ref.at[b], loss_ref.at[b], ls_sem.at[0], lr_sem.at[b], at(section=sender)).wait_recv()


def finish(scale, out_ref, sums_ref, tissue_ref, result_ref, loss_ref, sem):
    move = pltpu.make_async_copy(out_ref, result_ref, sem)
    move.start()
    width = loss_ref.shape[-1]
    loss_ref[...] = tissue_ref[...].astype(jnp.float32) * (sums_ref[...][:, :, 0, :width] * scale)
    move.wait()


def local(features, conv_weight, tissue):
    S = lax.axis_size("section")
    n_col = lax.axis_size("col")
    M, R, CL, C = features.shape
    halo = DILATION_RATE * S
    NR, NC = R + halo, CL + 2 * halo
    pairs = S // 2
    rows_max = (NR - DILATION_RATE) * NC
    cfg = (S, M, R, CL, C, n_col, halo, NR, NC)
    anyspec = pl.BlockSpec(memory_space=pl.ANY)
    dma = pltpu.SemaphoreType.DMA
    act = pltpu.VMEM(((NR + 2 * DILATION_RATE) * NC, C), jnp.bfloat16)
    features = pltpu.with_memory_space_constraint(features, pltpu.HBM)
    kernels = pltpu.with_memory_space_constraint(conv_weight.reshape(TAPS, TAPS, C, C), pltpu.HBM)
    out, sums = pl.pallas_call(
        functools.partial(kernel, cfg),
        out_shape=(
            jax.ShapeDtypeStruct((M, R, CL, C), jnp.bfloat16),
            jax.ShapeDtypeStruct((M, R, 1, 128), jnp.float32),
        ),
        in_specs=[pl.BlockSpec(memory_space=pltpu.HBM)] * 2,
        out_specs=(anyspec, anyspec),
        scratch_shapes=[
            pltpu.VMEM((NR, CL, C), jnp.bfloat16),
            pltpu.VMEM((NR * halo, C), jnp.bfloat16),
            pltpu.VMEM((NR * halo, C), jnp.bfloat16),
            pltpu.VMEM((R * halo, C), jnp.bfloat16),
            pltpu.VMEM((R * halo, C), jnp.bfloat16),
            pltpu.VMEM((S, TAPS, TAPS, C, C), jnp.bfloat16),
            act, act, act, act,
            pltpu.VMEM((rows_max, C), jnp.float32),
            pltpu.VMEM((rows_max, C), jnp.float32),
            pltpu.VMEM((S, NR, CL, C), jnp.bfloat16),
            pltpu.VMEM((S, NR, 1, 128), jnp.float32),
            dma((5,)), dma((5,)),
            dma((pairs, TAPS, 9)), dma((pairs, TAPS, 9)),
            dma((TAPS,)), dma((TAPS,)),
            pltpu.SemaphoreType.REGULAR,
            dma((S, 2)), dma((M, 2)),
            dma((S,)), dma((M,)),
            dma((7,)),
        ],
        compiler_params=pltpu.CompilerParams(
            collective_id=0, has_side_effects=True, vmem_limit_bytes=40 * 1024 * 1024
        ),
    )(features, kernels)
    result, loss = pl.pallas_call(
        functools.partial(finish, 1.0 / C),
        out_shape=(
            jax.ShapeDtypeStruct((M, R, CL, C), jnp.bfloat16),
            jax.ShapeDtypeStruct((M, R, CL), jnp.float32),
        ),
        in_specs=[anyspec, pl.BlockSpec(memory_space=pltpu.VMEM), pl.BlockSpec(memory_space=pltpu.VMEM)],
        out_specs=(pl.BlockSpec(memory_space=pltpu.HBM), pl.BlockSpec(memory_space=pltpu.VMEM)),
        scratch_shapes=[dma],
        compiler_params=pltpu.CompilerParams(vmem_limit_bytes=4 * 1024 * 1024),
    )(out, sums, tissue)
    return result[None], loss[None]


def solution(mesh):
    return jax.shard_map(
        local,
        mesh=mesh,
        in_specs=(
            P(None, "row", "col", None),
            P("section", None, None, None, None),
            P(None, "row", "col"),
        ),
        out_specs=(P("section", None, "row", "col", None), P("section", None, "row", "col")),
        check_vma=False,
    )
```

```python
import functools

import jax
import jax.numpy as jnp
from jax import lax
from jax.experimental import pallas as pl
from jax.experimental.pallas import tpu as pltpu
from jax.sharding import PartitionSpec as P

DILATION_RATE = 2
TAPS = 3
ORDER = (1, 0, 2)
residual_scale = 0.8
DIRECT_ROWS = 32
EARLY = 3
GO = 2
MESH = pl.DeviceIdType.MESH
OWN, DIRECT, ROW, COL, DIAG = range(5)


def kernel(cfg, f_ref, w_ref, out_ref, loss_ref, fwin, lstrip, rstrip, lpack, rpack, wall, a0, a1, b0, b1, s0, s1, stage, stage2, lstage,
           hs_sem, hr_sem, ws_sem, wr_sem, ks_sem, kr_sem, go_sem, os_sem, or_sem, ls_sem, lr_sem, loc_sem):
    S, M, R, CL, C, n_col, halo, NR, NC = cfg
    me = lax.axis_index("section")
    col = lax.axis_index("col")
    row = lax.axis_index("row")
    micro = lax.rem(me, M)
    group = S // M
    replica = me // M
    low = lax.rem(me, 2)
    sib = me + 1 - 2 * low
    pairs = S // 2
    my_pair = me // 2
    other_row = 1 - row
    mate = col + 1 - 2 * lax.rem(col, 2)
    has_left = col > 0
    has_right = col < n_col - 1
    quarter = C // 4
    direct = DIRECT_ROWS * quarter // 64
    my_q = 2 * row + lax.rem(col, 2)

    def at(section=None, c=None, r=None):
        return {
            "section": me if section is None else section,
            "col": col if c is None else c,
            "row": row if r is None else r,
        }

    barrier = pltpu.get_barrier_semaphore()

    def hello(dev):
        pl.semaphore_signal(barrier, inc=1, device_id=dev, device_id_type=MESH)

    for d in range(1, S):
        hello(at(section=lax.rem(me + d, S)))
    hello(at(r=other_row))

    @pl.when(has_left)
    def _():
        hello(at(c=col - 1))
        hello(at(c=col - 1, r=other_row))

    @pl.when(has_right)
    def _():
        hello(at(c=col + 1))
        hello(at(c=col + 1, r=other_row))

    own_w = [pltpu.make_async_copy(w_ref.at[:, kx], wall.at[me, kx], loc_sem.at[kx]) for kx in range(TAPS)]
    own_f = pltpu.make_async_copy(
        f_ref.at[micro],
        fwin.at[pl.ds(row * halo, R)],
        loc_sem.at[3],
    )
    own_f.start()
    for kx in ORDER:
        own_w[kx].start()

    zeros = jnp.zeros((DILATION_RATE * NC, C), jnp.bfloat16)
    for ref in (a0, b0, b1, a1):
        ref[0 : DILATION_RATE * NC, :] = zeros
        ref[(DILATION_RATE + NR) * NC :, :] = zeros

    own_f.wait()
    edge = fwin[pl.ds(row * halo, R)].astype(jnp.float32)
    lpack[...] = edge[:, :halo, :].reshape(R * halo, C).astype(jnp.bfloat16)
    rpack[...] = edge[:, CL - halo :, :].reshape(R * halo, C).astype(jnp.bfloat16)

    greeted = 1 + (S - 1) + 2 * has_left.astype(jnp.int32) + 2 * has_right.astype(jnp.int32)
    pl.semaphore_wait(barrier, greeted)

    def remote(src, dst, s_sem, r_sem, dev):
        return pltpu.make_async_remote_copy(
            src_ref=src, dst_ref=dst, send_sem=s_sem, recv_sem=r_sem,
            device_id=dev, device_id_type=MESH,
        )

    def twin(k):
        a, b, res, bit = my_pair, k, 0, 1
        while bit < pairs:
            res = res + bit * lax.rem(a // bit + b // bit, 2)
            bit *= 2
        return 2 * res + low

    def rows_of(kind):
        if kind == OWN:
            return my_q * quarter, quarter
        if kind == DIRECT:
            return (3 - my_q) * quarter, direct
        if kind == ROW:
            return (my_q + 2 - 4 * row) * quarter, quarter
        if kind == COL:
            return (my_q + 1 - 2 * lax.rem(col, 2)) * quarter, quarter
        if kind == DIAG:
            return (3 - my_q) * quarter + direct, quarter - direct

    routed = (ROW, COL, DIAG) if direct < quarter else (ROW, COL)

    def part(kind):
        start, size = rows_of(kind)
        return pl.ds(pl.multiple_of(start, 16), size)

    def sent_part(kind):
        if kind == DIAG:
            return pl.ds(pl.multiple_of(my_q * quarter + direct, 16), quarter - direct)
        return part(OWN)

    def give(k, kx, kind):
        piece = part(kind)
        return remote(w_ref.at[:, kx, piece], wall.at[me, kx, :, piece],
                      ws_sem.at[k, kx, kind], wr_sem.at[k, kx, kind], at(section=twin(k)))

    def forward(l, k, kx, kind):
        piece = sent_part(kind)
        dev = {ROW: at(r=other_row), COL: at(c=mate), DIAG: at(c=mate, r=other_row)}[kind]
        slot = wall.at[l, kx, :, piece]
        return remote(slot, slot, ws_sem.at[k, kx, kind], wr_sem.at[k, kx, kind], dev)

    def arrival(l, k, kx, kind):
        slot = wall.at[l, kx, :, part(kind)]
        return remote(slot, slot, ws_sem.at[k, kx, kind], wr_sem.at[k, kx, kind], at(section=twin(k)))

    SHARES = (OWN, ROW, COL, DIAG)

    def share(l, k, kx, kind):
        start = rows_of(DIRECT)[0] if kind == DIAG else rows_of(kind)[0]
        slot = wall.at[l, kx, :, pl.ds(pl.multiple_of(start, 16), quarter)]
        n = 5 + SHARES.index(kind)
        return remote(slot, slot, ws_sem.at[k, kx, n], wr_sem.at[k, kx, n], at(section=sib))

    def to_sib(kx):
        return remote(w_ref.at[:, kx], wall.at[me, kx], ks_sem.at[kx], kr_sem.at[kx], at(section=sib))

    def send_own(kind, js):
        for j in js:
            for k in range(1, pairs):
                give(k, ORDER[j], kind).start()

    def own_sent(kind, js):
        for j in js:
            for k in range(1, pairs):
                give(k, ORDER[j], kind).wait_send()

    def relay(l, kx):
        for k in range(1, pairs):
            @pl.when(twin(k) == l)
            def _(k=k):
                arrival(l, k, kx, OWN).wait_recv()
                for kind in routed:
                    forward(l, k, kx, kind).start()
                share(l, k, kx, OWN).start()

    def gather(l, kx):
        for k in range(1, pairs):
            @pl.when(twin(k) == l)
            def _(k=k):
                for kind in (COL, ROW):
                    arrival(l, k, kx, kind).wait_recv()
                    share(l, k, kx, kind).start()
                arrival(l, k, kx, DIRECT).wait_recv()
                if DIAG in routed:
                    arrival(l, k, kx, DIAG).wait_recv()
                share(l, k, kx, DIAG).start()

    def complete(l, kx, gathered):
        @pl.when(me == l)
        def _():
            own_w[kx].wait()

        @pl.when(sib == l)
        def _():
            to_sib(kx).wait_recv()

        if gathered is None:
            gather(l, kx)
        elif gathered is not True:
            pl.when(jnp.logical_not(gathered))(lambda: gather(l, kx))
        for k in range(1, pairs):
            @pl.when(twin(k) + 1 - 2 * low == l)
            def _(k=k):
                for kind in SHARES:
                    share(l, k, kx, kind).wait_recv()

    every = range(TAPS)

    @pl.when(low == 0)
    def _():
        send_own(OWN, every)
        send_own(DIRECT, every[:EARLY])


    def strip(start, count):
        return pl.ds(pl.multiple_of(start * halo, 16), count * halo)

    out_row, in_row = (1 - row) * (R - halo), row * R
    here, across, into = strip(row * halo, R), strip(out_row, halo), strip(in_row, halo)
    to_left = remote(lpack, rstrip.at[here], hs_sem.at[0], hr_sem.at[0], at(c=col - 1))
    to_right = remote(rpack, lstrip.at[here], hs_sem.at[1], hr_sem.at[1], at(c=col + 1))
    to_row = remote(f_ref.at[micro, pl.ds(out_row, halo)], fwin.at[pl.ds(in_row, halo)], hs_sem.at[2], hr_sem.at[2], at(r=other_row))
    to_dl = remote(lpack.at[across], rstrip.at[into], hs_sem.at[3], hr_sem.at[3], at(c=col - 1, r=other_row))
    to_dr = remote(rpack.at[across], lstrip.at[into], hs_sem.at[4], hr_sem.at[4], at(c=col + 1, r=other_row))
    to_row.start()

    @pl.when(has_left)
    def _():
        to_left.start()
        to_dl.start()

    @pl.when(has_right)
    def _():
        to_right.start()
        to_dr.start()

    for kx in ORDER:
        to_sib(kx).start()

    def first_even(j):
        kx = ORDER[j]
        relay(0, kx)
        if pairs > 1:
            pl.when(my_pair == 0)(lambda: relay(2, kx))

    @pl.when(low == 0)
    def _():
        own_sent(OWN, every[:GO])
        pl.semaphore_signal(go_sem, inc=1, device_id=at(section=sib), device_id_type=MESH)

    @pl.when(low == 1)
    def _():
        pl.semaphore_wait(go_sem, 1)
        send_own(OWN, every)
        send_own(DIRECT, every)

    first_even(0)
    first_even(1)

    def in_map_only(v):
        return jnp.concatenate(
            [
                jnp.where(has_left, v[:, :halo], 0.0),
                v[:, halo : halo + CL],
                jnp.where(has_right, v[:, halo + CL :], 0.0),
            ],
            axis=1,
        )

    def fill(start, count):
        for i in range(0, count, 4):
            at_row = start + i
            side = strip(at_row, 4)
            v = jnp.concatenate(
                [
                    jnp.where(has_left, lstrip[side, :].astype(jnp.float32).reshape(4, halo, C), 0.0),
                    fwin[pl.ds(at_row, 4)].astype(jnp.float32),
                    jnp.where(has_right, rstrip[side, :].astype(jnp.float32).reshape(4, halo, C), 0.0),
                ],
                axis=1,
            )
            place = pl.ds(pl.multiple_of((at_row + DILATION_RATE) * NC, 16), 4 * NC)
            a0[place, :] = v.reshape(4 * NC, C).astype(jnp.bfloat16)

    def sides_in():
        @pl.when(has_left)
        def _():
            to_left.wait_send()
            to_right.wait_recv()

        @pl.when(has_right)
        def _():
            to_right.wait_send()
            to_left.wait_recv()

        fill(row * halo, R)

    def rows_come_in():
        to_row.wait()

        @pl.when(has_left)
        def _():
            to_dl.wait_send()
            to_dr.wait_recv()

        @pl.when(has_right)
        def _():
            to_dr.wait_send()
            to_dl.wait_recv()

        fill((1 - row) * R, halo)

    sides_in()
    first_even(2)
    pl.when(low == 0)(lambda: send_own(DIRECT, every[EARLY:]))
    split_first = halo + DILATION_RATE <= R
    if not split_first:
        rows_come_in()

    def after(l, j):
        if pairs > 1:
            if l == 0 and j == 2:
                def early():
                    gather(2, ORDER[0])
                    gather(2, ORDER[1])
                pl.when(my_pair == 0)(early)
            if l == 1 and j == 0:
                pl.when(my_pair == 0)(lambda: relay(3, ORDER[0]))
            if l == 1 and j == 1:
                def late():
                    gather(2, ORDER[2])
                    relay(3, ORDER[1])
                pl.when(my_pair == 0)(late)
            if l == 2 and j == 0:
                pl.when(my_pair == 0)(lambda: relay(3, ORDER[2]))
        if j == 2 and l + 2 < S and l + 2 >= 2:
            t = l + 2
            for kk in ORDER:
                if t in (2, 3):
                    pl.when(my_pair > 0)(lambda t=t, kk=kk: relay(t, kk))
                else:
                    relay(t, kk)

    def step_done(l, j, q):
        if l == 0 and q == 0:
            pl.when(my_pair > 0)(lambda: relay(1, ORDER[j]))
        if q == 1:
            after(l, j)

    def out_copy(l, h):
        n = NR - DILATION_RATE * (l + 1)
        half = R // 2
        place = pl.ds(pl.multiple_of((row if h == 0 else other_row) * half, half), half)
        src = stage.at[l, pl.ds(row * (n - R) + (row if h == 0 else other_row) * half, half)]
        return src, out_ref.at[micro, place]

    def loss_copy(l):
        return lstage.at[l], loss_ref.at[micro]

    def out_send(l, h):
        src, dst = out_copy(l, h)
        return remote(src, dst, os_sem.at[l, h], or_sem.at[micro, h], at(section=l))

    def loss_send(l):
        src, dst = loss_copy(l)
        return remote(src, dst, ls_sem.at[l], lr_sem.at[micro], at(section=l))

    def out_keep(l, h):
        src, dst = out_copy(l, h)
        return pltpu.make_async_copy(src, dst, loc_sem.at[4 + h])

    def loss_keep(l):
        src, dst = loss_copy(l)
        return pltpu.make_async_copy(src, dst, loc_sem.at[6])

    def sends(l):
        return jnp.logical_and(replica == l % group, me != l)

    def keeps(l):
        return jnp.logical_and(replica == l % group, me == l)

    def loss_of(l):
        n = NR - DILATION_RATE * (l + 1)
        own = pl.ds(row * (n - R), R)
        d = stage[l, own].astype(jnp.float32) - stage2[l, own].astype(jnp.float32)
        d = jnp.sum(d * d, axis=-1, keepdims=True)
        lstage[l] = jnp.sum(jnp.where(eye, d, 0.0), axis=1, keepdims=True)
        pl.when(sends(l))(lambda: loss_send(l).start())
        pl.when(keeps(l))(lambda: loss_keep(l).start())

    eye = lax.broadcasted_iota(jnp.int32, (1, CL, 128), 1) == lax.broadcasted_iota(jnp.int32, (1, CL, 128), 2)

    for l in range(S):
        n = NR - DILATION_RATE * (l + 1)
        r0 = row * (NR - n)
        chunk = n // 2
        m = chunk * NC
        cur, nxt = ((a0, a1), (b0, b1))[l % 2], ((a0, a1), (b0, b1))[(l + 1) % 2]
        sums = (s0, s1)
        shared = l == 0
        steps = [(j, q) for q in range(2) for j in range(TAPS)] if shared else [(j, q) for j in range(TAPS) for q in range(2)]
        for j, q in steps:
                kx = ORDER[j]
                if q == 0:
                    complete(l, kx, (my_pair == 0) if l == 2 else None)
                if shared and split_first and (j, q) == (0, 1):
                    rows_come_in()
                w = wall[l, kx].reshape(TAPS * C, C)
                place = row if q == 0 else other_row
                base = r0 + place * chunk
                keep = pl.ds(q * m, m)
                centre = pl.ds(pl.multiple_of((base + DILATION_RATE) * NC, 16), m)
                products = []
                for mem in range(1 if shared else 2):
                    lhs = jnp.concatenate(
                        [cur[mem][pl.ds(pl.multiple_of((base + DILATION_RATE * ky) * NC, 16), m), :] for ky in range(TAPS)],
                        axis=1,
                    )
                    products.append(jnp.dot(lhs, w, preferred_element_type=jnp.float32))
                if shared:
                    products.append(products[0])
                if kx == 1:
                    for mem in range(1 if shared else 2):
                        sums[mem][keep, :] = products[mem]
                    step_done(l, j, q)
                    continue
                shift = DILATION_RATE if kx == 0 else m - DILATION_RATE
                moved = [pltpu.roll(products[mem], shift if mem == 0 else m - shift, 0) for mem in range(2)]
                if kx == 0:
                    before = [sums[0 if shared else mem][keep, :] for mem in range(2)]
                    for mem in range(2):
                        sums[mem][keep, :] = before[mem] + moved[mem]
                    step_done(l, j, q)
                    continue
                for mem in range(2):
                    conv = sums[mem][keep, :] + moved[mem]
                    res = cur[0 if shared else mem][centre, :].astype(jnp.float32)
                    y = residual_scale * (res + jnp.maximum(conv, 0.0))
                    y = in_map_only(y.reshape(chunk, NC, C))
                    if l < S - 1:
                        nxt[mem][centre, :] = y.reshape(m, C).astype(jnp.bfloat16)
                    kept = stage if mem == 0 else stage2
                    kept[l, pl.ds(place * chunk, chunk)] = y[:, halo : halo + CL, :].astype(jnp.bfloat16)

                @pl.when(sends(l))
                def _(l=l, q=q):
                    out_send(l, q).start()

                @pl.when(keeps(l))
                def _(l=l, q=q):
                    out_keep(l, q).start()
                if q == 1:
                    if l < 2 and S > 2:
                        pl.when(my_pair > 0)(lambda: loss_of(l))
                    else:
                        loss_of(l)
                    if l == 2:
                        def earlier():
                            loss_of(0)
                            loss_of(1)
                        pl.when(my_pair == 0)(earlier)
                step_done(l, j, q)

    own_sent(OWN, every[GO:])
    own_sent(DIRECT, every)

    @pl.when(low == 1)
    def _():
        own_sent(OWN, every[:GO])

    for k in range(1, pairs):
        for kx in ORDER:
            for kind in routed:
                forward(twin(k), k, kx, kind).wait_send()
            for kind in SHARES:
                share(twin(k), k, kx, kind).wait_send()
    for kx in ORDER:
        to_sib(kx).wait_send()

    for l in range(S):
        @pl.when(sends(l))
        def _(l=l):
            out_send(l, 0).wait_send()
            out_send(l, 1).wait_send()
            loss_send(l).wait_send()

        @pl.when(keeps(l))
        def _(l=l):
            out_keep(l, 0).wait()
            out_keep(l, 1).wait()
            loss_keep(l).wait()

    for b in range(M):
        sender = b + M * lax.rem(me, group)

        @pl.when(sender != me)
        def _(b=b, sender=sender):
            for h in range(2):
                half = R // 2
                place = pl.ds(pl.multiple_of((row if h == 0 else other_row) * half, half), half)
                dst = out_ref.at[b, place]
                remote(dst, dst, os_sem.at[0, h], or_sem.at[b, h], at(section=sender)).wait_recv()
            remote(loss_ref.at[b], loss_ref.at[b], ls_sem.at[0], lr_sem.at[b], at(section=sender)).wait_recv()


def finish(scale, out_ref, sums_ref, tissue_ref, result_ref, loss_ref, sem):
    move = pltpu.make_async_copy(out_ref, result_ref, sem)
    move.start()
    width = loss_ref.shape[-1]
    loss_ref[...] = tissue_ref[...].astype(jnp.float32) * (sums_ref[...][:, :, 0, :width] * scale)
    move.wait()


def local(features, conv_weight, tissue):
    S = lax.axis_size("section")
    n_col = lax.axis_size("col")
    M, R, CL, C = features.shape
    halo = DILATION_RATE * S
    NR, NC = R + halo, CL + 2 * halo
    pairs = S // 2
    rows_max = (NR - DILATION_RATE) * NC
    cfg = (S, M, R, CL, C, n_col, halo, NR, NC)
    anyspec = pl.BlockSpec(memory_space=pl.ANY)
    dma = pltpu.SemaphoreType.DMA
    act = pltpu.VMEM(((NR + 2 * DILATION_RATE) * NC, C), jnp.bfloat16)
    features = pltpu.with_memory_space_constraint(features, pltpu.HBM)
    kernels = pltpu.with_memory_space_constraint(conv_weight.reshape(TAPS, TAPS, C, C), pltpu.HBM)
    out, sums = pl.pallas_call(
        functools.partial(kernel, cfg),
        out_shape=(
            jax.ShapeDtypeStruct((M, R, CL, C), jnp.bfloat16),
            jax.ShapeDtypeStruct((M, R, 1, 128), jnp.float32),
        ),
        in_specs=[pl.BlockSpec(memory_space=pltpu.HBM)] * 2,
        out_specs=(anyspec, anyspec),
        scratch_shapes=[
            pltpu.VMEM((NR, CL, C), jnp.bfloat16),
            pltpu.VMEM((NR * halo, C), jnp.bfloat16),
            pltpu.VMEM((NR * halo, C), jnp.bfloat16),
            pltpu.VMEM((R * halo, C), jnp.bfloat16),
            pltpu.VMEM((R * halo, C), jnp.bfloat16),
            pltpu.VMEM((S, TAPS, TAPS, C, C), jnp.bfloat16),
            act, act, act, act,
            pltpu.VMEM((rows_max, C), jnp.float32),
            pltpu.VMEM((rows_max, C), jnp.float32),
            pltpu.VMEM((S, NR, CL, C), jnp.bfloat16),
            pltpu.VMEM((S, NR, CL, C), jnp.bfloat16),
            pltpu.VMEM((S, R, 1, 128), jnp.float32),
            dma((5,)), dma((5,)),
            dma((pairs, TAPS, 9)), dma((pairs, TAPS, 9)),
            dma((TAPS,)), dma((TAPS,)),
            pltpu.SemaphoreType.REGULAR,
            dma((S, 2)), dma((M, 2)),
            dma((S,)), dma((M,)),
            dma((7,)),
        ],
        compiler_params=pltpu.CompilerParams(
            collective_id=0, has_side_effects=True, vmem_limit_bytes=40 * 1024 * 1024
        ),
    )(features, kernels)
    result, loss = pl.pallas_call(
        functools.partial(finish, 1.0 / C),
        out_shape=(
            jax.ShapeDtypeStruct((M, R, CL, C), jnp.bfloat16),
            jax.ShapeDtypeStruct((M, R, CL), jnp.float32),
        ),
        in_specs=[anyspec, pl.BlockSpec(memory_space=pltpu.VMEM), pl.BlockSpec(memory_space=pltpu.VMEM)],
        out_specs=(pl.BlockSpec(memory_space=pltpu.HBM), pl.BlockSpec(memory_space=pltpu.VMEM)),
        scratch_shapes=[dma],
        compiler_params=pltpu.CompilerParams(vmem_limit_bytes=4 * 1024 * 1024),
    )(out, sums, tissue)
    return result[None], loss[None]


def solution(mesh):
    return jax.shard_map(
        local,
        mesh=mesh,
        in_specs=(
            P(None, "row", "col", None),
            P("section", None, None, None, None),
            P(None, "row", "col"),
        ),
        out_specs=(P("section", None, "row", "col", None), P("section", None, "row", "col")),
        check_vma=False,
    )
```

```python
import functools

import jax
import jax.numpy as jnp
from jax import lax
from jax.experimental import pallas as pl
from jax.experimental.pallas import tpu as pltpu
from jax.sharding import PartitionSpec as P

DILATION_RATE = 2
TAPS = 3
ORDER = (1, 0, 2)
residual_scale = 0.8
DIRECT_ROWS = (48, 64)
EARLY = 3
GO = 1
HOOKS = {
    (0, 2): (("gather", 2, 0), ("gather", 2, 1)),
    (1, 0): (("relay", 3, 0),),
    (1, 1): (("gather", 2, 2), ("relay", 3, 1)),
    (2, 0): (("relay", 3, 2),),
}
MESH = pl.DeviceIdType.MESH
OWN, DIRECT, ROW, COL, DIAG = range(5)


def kernel(cfg, f_ref, w_ref, out_ref, loss_ref, fwin, lstrip, rstrip, lpack, rpack, wall, a0, a1, b0, b1, s0, s1, stage, stage2, lstage,
           hs_sem, hr_sem, ws_sem, wr_sem, ks_sem, kr_sem, go_sem, os_sem, or_sem, ls_sem, lr_sem, loc_sem):
    S, M, R, CL, C, n_col, halo, NR, NC = cfg
    me = lax.axis_index("section")
    col = lax.axis_index("col")
    row = lax.axis_index("row")
    micro = lax.rem(me, M)
    group = S // M
    replica = me // M
    low = lax.rem(me, 2)
    sib = me + 1 - 2 * low
    pairs = S // 2
    my_pair = me // 2
    other_row = 1 - row
    mate = col + 1 - 2 * lax.rem(col, 2)
    has_left = col > 0
    has_right = col < n_col - 1
    quarter = C // 4
    directs = [rows * quarter // 64 for rows in DIRECT_ROWS]
    my_q = 2 * row + lax.rem(col, 2)

    def at(section=None, c=None, r=None):
        return {
            "section": me if section is None else section,
            "col": col if c is None else c,
            "row": row if r is None else r,
        }

    barrier = pltpu.get_barrier_semaphore()

    def hello(dev):
        pl.semaphore_signal(barrier, inc=1, device_id=dev, device_id_type=MESH)

    for d in range(1, S):
        hello(at(section=lax.rem(me + d, S)))
    hello(at(r=other_row))

    @pl.when(has_left)
    def _():
        hello(at(c=col - 1))
        hello(at(c=col - 1, r=other_row))

    @pl.when(has_right)
    def _():
        hello(at(c=col + 1))
        hello(at(c=col + 1, r=other_row))

    own_w = [pltpu.make_async_copy(w_ref.at[:, kx], wall.at[me, kx], loc_sem.at[kx]) for kx in range(TAPS)]
    own_f = pltpu.make_async_copy(
        f_ref.at[micro],
        fwin.at[pl.ds(row * halo, R)],
        loc_sem.at[3],
    )
    own_f.start()
    for kx in ORDER:
        own_w[kx].start()

    zeros = jnp.zeros((DILATION_RATE * NC, C), jnp.bfloat16)
    for ref in (a0, b0, b1, a1):
        ref[0 : DILATION_RATE * NC, :] = zeros
        ref[(DILATION_RATE + NR) * NC :, :] = zeros

    own_f.wait()
    edge = fwin[pl.ds(row * halo, R)].astype(jnp.float32)
    lpack[...] = edge[:, :halo, :].reshape(R * halo, C).astype(jnp.bfloat16)
    rpack[...] = edge[:, CL - halo :, :].reshape(R * halo, C).astype(jnp.bfloat16)

    greeted = 1 + (S - 1) + 2 * has_left.astype(jnp.int32) + 2 * has_right.astype(jnp.int32)
    pl.semaphore_wait(barrier, greeted)

    def remote(src, dst, s_sem, r_sem, dev):
        return pltpu.make_async_remote_copy(
            src_ref=src, dst_ref=dst, send_sem=s_sem, recv_sem=r_sem,
            device_id=dev, device_id_type=MESH,
        )

    def twin(k):
        a, b, res, bit = my_pair, k, 0, 1
        while bit < pairs:
            res = res + bit * lax.rem(a // bit + b // bit, 2)
            bit *= 2
        return 2 * res + low

    def rows_of(kind, direct=None):
        if kind == OWN:
            return my_q * quarter, quarter
        if kind == DIRECT:
            return (3 - my_q) * quarter, direct
        if kind == ROW:
            return (my_q + 2 - 4 * row) * quarter, quarter
        if kind == COL:
            return (my_q + 1 - 2 * lax.rem(col, 2)) * quarter, quarter
        if kind == DIAG:
            return (3 - my_q) * quarter + direct, quarter - direct

    def direct_of(l):
        return directs[l % 2]

    def routed(l):
        return (ROW, COL, DIAG) if direct_of(l) < quarter else (ROW, COL)

    def part(kind, direct):
        start, size = rows_of(kind, direct)
        return pl.ds(pl.multiple_of(start, 16), size)

    def sent_part(kind, direct):
        if kind == DIAG:
            return pl.ds(pl.multiple_of(my_q * quarter + direct, 16), quarter - direct)
        return part(OWN, direct)

    def give(k, kx, kind, direct):
        piece = part(kind, direct)
        return remote(w_ref.at[:, kx, piece], wall.at[me, kx, :, piece],
                      ws_sem.at[k, kx, kind], wr_sem.at[k, kx, kind], at(section=twin(k)))

    def forward(l, k, kx, kind):
        piece = sent_part(kind, direct_of(l))
        dev = {ROW: at(r=other_row), COL: at(c=mate), DIAG: at(c=mate, r=other_row)}[kind]
        slot = wall.at[l, kx, :, piece]
        return remote(slot, slot, ws_sem.at[k, kx, kind], wr_sem.at[k, kx, kind], dev)

    def arrival(l, k, kx, kind):
        slot = wall.at[l, kx, :, part(kind, direct_of(l))]
        return remote(slot, slot, ws_sem.at[k, kx, kind], wr_sem.at[k, kx, kind], at(section=twin(k)))

    SHARES = (OWN, ROW, COL, DIAG)

    def share(l, k, kx, kind):
        start = rows_of(DIRECT, directs[0])[0] if kind == DIAG else rows_of(kind)[0]
        slot = wall.at[l, kx, :, pl.ds(pl.multiple_of(start, 16), quarter)]
        n = 5 + SHARES.index(kind)
        return remote(slot, slot, ws_sem.at[k, kx, n], wr_sem.at[k, kx, n], at(section=sib))

    def to_sib(kx):
        return remote(w_ref.at[:, kx], wall.at[me, kx], ks_sem.at[kx], kr_sem.at[kx], at(section=sib))

    def send_own(kind, js):
        for first, direct in enumerate(directs):
            @pl.when(low == first)
            def _(direct=direct):
                for j in js:
                    for k in range(1, pairs):
                        give(k, ORDER[j], kind, direct).start()

    def own_sent(kind, js):
        for first, direct in enumerate(directs):
            @pl.when(low == first)
            def _(direct=direct):
                for j in js:
                    for k in range(1, pairs):
                        give(k, ORDER[j], kind, direct).wait_send()

    def relay(l, kx):
        for k in range(1, pairs):
            @pl.when(twin(k) == l)
            def _(k=k):
                arrival(l, k, kx, OWN).wait_recv()
                for kind in routed(l):
                    forward(l, k, kx, kind).start()
                share(l, k, kx, OWN).start()

    def gather(l, kx):
        for k in range(1, pairs):
            @pl.when(twin(k) == l)
            def _(k=k):
                for kind in (COL, ROW):
                    arrival(l, k, kx, kind).wait_recv()
                    share(l, k, kx, kind).start()
                arrival(l, k, kx, DIRECT).wait_recv()
                if DIAG in routed(l):
                    arrival(l, k, kx, DIAG).wait_recv()
                share(l, k, kx, DIAG).start()

    def complete(l, kx, gathered):
        @pl.when(me == l)
        def _():
            own_w[kx].wait()

        @pl.when(sib == l)
        def _():
            to_sib(kx).wait_recv()

        if gathered is None:
            gather(l, kx)
        elif gathered is not True:
            pl.when(jnp.logical_not(gathered))(lambda: gather(l, kx))
        for k in range(1, pairs):
            @pl.when(twin(k) + 1 - 2 * low == l)
            def _(k=k):
                for kind in SHARES:
                    share(l, k, kx, kind).wait_recv()

    every = range(TAPS)

    @pl.when(low == 0)
    def _():
        send_own(OWN, every)
        send_own(DIRECT, every[:EARLY])


    def strip(start, count):
        return pl.ds(pl.multiple_of(start * halo, 16), count * halo)

    out_row, in_row = (1 - row) * (R - halo), row * R
    here, across, into = strip(row * halo, R), strip(out_row, halo), strip(in_row, halo)
    to_left = remote(lpack, rstrip.at[here], hs_sem.at[0], hr_sem.at[0], at(c=col - 1))
    to_right = remote(rpack, lstrip.at[here], hs_sem.at[1], hr_sem.at[1], at(c=col + 1))
    to_row = remote(f_ref.at[micro, pl.ds(out_row, halo)], fwin.at[pl.ds(in_row, halo)], hs_sem.at[2], hr_sem.at[2], at(r=other_row))
    to_dl = remote(lpack.at[across], rstrip.at[into], hs_sem.at[3], hr_sem.at[3], at(c=col - 1, r=other_row))
    to_dr = remote(rpack.at[across], lstrip.at[into], hs_sem.at[4], hr_sem.at[4], at(c=col + 1, r=other_row))
    to_row.start()

    @pl.when(has_left)
    def _():
        to_left.start()
        to_dl.start()

    @pl.when(has_right)
    def _():
        to_right.start()
        to_dr.start()

    for kx in ORDER:
        to_sib(kx).start()

    def first_even(j):
        kx = ORDER[j]
        relay(0, kx)
        if pairs > 1:
            pl.when(my_pair == 0)(lambda: relay(2, kx))

    @pl.when(low == 0)
    def _():
        own_sent(OWN, every[:GO])
        pl.semaphore_signal(go_sem, inc=1, device_id=at(section=sib), device_id_type=MESH)

    @pl.when(low == 1)
    def _():
        pl.semaphore_wait(go_sem, 1)
        send_own(OWN, every)
        send_own(DIRECT, every)

    first_even(0)
    first_even(1)

    def in_map_only(v):
        return jnp.concatenate(
            [
                jnp.where(has_left, v[:, :halo], 0.0),
                v[:, halo : halo + CL],
                jnp.where(has_right, v[:, halo + CL :], 0.0),
            ],
            axis=1,
        )

    def fill(start, count):
        for i in range(0, count, 4):
            at_row = start + i
            side = strip(at_row, 4)
            v = jnp.concatenate(
                [
                    jnp.where(has_left, lstrip[side, :].astype(jnp.float32).reshape(4, halo, C), 0.0),
                    fwin[pl.ds(at_row, 4)].astype(jnp.float32),
                    jnp.where(has_right, rstrip[side, :].astype(jnp.float32).reshape(4, halo, C), 0.0),
                ],
                axis=1,
            )
            place = pl.ds(pl.multiple_of((at_row + DILATION_RATE) * NC, 16), 4 * NC)
            a0[place, :] = v.reshape(4 * NC, C).astype(jnp.bfloat16)

    def sides_in():
        @pl.when(has_left)
        def _():
            to_left.wait_send()
            to_right.wait_recv()

        @pl.when(has_right)
        def _():
            to_right.wait_send()
            to_left.wait_recv()

        fill(row * halo, R)

    def rows_come_in():
        to_row.wait()

        @pl.when(has_left)
        def _():
            to_dl.wait_send()
            to_dr.wait_recv()

        @pl.when(has_right)
        def _():
            to_dr.wait_send()
            to_dl.wait_recv()

        fill((1 - row) * R, halo)

    sides_in()
    first_even(2)
    pl.when(low == 0)(lambda: send_own(DIRECT, every[EARLY:]))
    split_first = halo + DILATION_RATE <= R
    if not split_first:
        rows_come_in()

    def after(l, j):
        if pairs > 1:
            if (l, j) in HOOKS:
                def meanwhile():
                    for what, t, i in HOOKS[(l, j)]:
                        (gather if what == "gather" else relay)(t, ORDER[i])
                pl.when(my_pair == 0)(meanwhile)
        if j == 2 and l + 2 < S and l + 2 >= 2:
            t = l + 2
            for kk in ORDER:
                if t in (2, 3):
                    pl.when(my_pair > 0)(lambda t=t, kk=kk: relay(t, kk))
                else:
                    relay(t, kk)

    def step_done(l, mems, j, q):
        if l == 0 and q == 0:
            pl.when(my_pair > 0)(lambda: relay(1, ORDER[j]))
        if q == 1 and len(mems) == 2:
            after(l, j)
        elif (q, j) == (1, 2) and mems == (0,):
            after(l, 0)
            after(l, 1)
        elif (q, j) == (1, 2):
            after(l, 2)

    def out_copy(l, h):
        n = NR - DILATION_RATE * (l + 1)
        half = R // 2
        place = pl.ds(pl.multiple_of((row if h == 0 else other_row) * half, half), half)
        src = stage.at[l, pl.ds(row * (n - R) + (row if h == 0 else other_row) * half, half)]
        return src, out_ref.at[micro, place]

    def loss_copy(l):
        return lstage.at[l], loss_ref.at[micro]

    def out_send(l, h):
        src, dst = out_copy(l, h)
        return remote(src, dst, os_sem.at[l, h], or_sem.at[micro, h], at(section=l))

    def loss_send(l):
        src, dst = loss_copy(l)
        return remote(src, dst, ls_sem.at[l], lr_sem.at[micro], at(section=l))

    def out_keep(l, h):
        src, dst = out_copy(l, h)
        return pltpu.make_async_copy(src, dst, loc_sem.at[4 + h])

    def loss_keep(l):
        src, dst = loss_copy(l)
        return pltpu.make_async_copy(src, dst, loc_sem.at[6])

    def sends(l):
        return jnp.logical_and(replica == l % group, me != l)

    def keeps(l):
        return jnp.logical_and(replica == l % group, me == l)

    def loss_of(l):
        n = NR - DILATION_RATE * (l + 1)
        own = pl.ds(row * (n - R), R)
        d = stage[l, own].astype(jnp.float32) - stage2[l, own].astype(jnp.float32)
        d = jnp.sum(d * d, axis=-1, keepdims=True)
        lstage[l] = jnp.sum(jnp.where(eye, d, 0.0), axis=1, keepdims=True)
        pl.when(sends(l))(lambda: loss_send(l).start())
        pl.when(keeps(l))(lambda: loss_keep(l).start())

    eye = lax.broadcasted_iota(jnp.int32, (1, CL, 128), 1) == lax.broadcasted_iota(jnp.int32, (1, CL, 128), 2)

    for l in range(S):
        n = NR - DILATION_RATE * (l + 1)
        r0 = row * (NR - n)
        chunk = n // 2
        m = chunk * NC
        cur, nxt = ((a0, a1), (b0, b1))[l % 2], ((a0, a1), (b0, b1))[(l + 1) % 2]
        sums = (s0, s1)
        shared = l == 0
        both = (0, 1)
        if shared:
            steps = [(both, j, q) for q in range(2) for j in range(TAPS)]
        elif l < 2:
            steps = [(both, j, q) for j in range(TAPS) for q in range(2)]
        else:
            steps = [((mem,), j, q) for mem in both for j in range(TAPS) for q in range(2)]
        for mems, j, q in steps:
            kx = ORDER[j]
            if q == 0 and 0 in mems:
                complete(l, kx, (my_pair == 0) if l == 2 else None)
            if shared and split_first and (j, q) == (0, 1):
                rows_come_in()
            w = wall[l, kx].reshape(TAPS * C, C)
            place = row if q == 0 else other_row
            base = r0 + place * chunk
            keep = pl.ds(q * m, m)
            centre = pl.ds(pl.multiple_of((base + DILATION_RATE) * NC, 16), m)
            products = {}
            for mem in (0,) if shared else mems:
                lhs = jnp.concatenate(
                    [cur[mem][pl.ds(pl.multiple_of((base + DILATION_RATE * ky) * NC, 16), m), :] for ky in range(TAPS)],
                    axis=1,
                )
                products[mem] = jnp.dot(lhs, w, preferred_element_type=jnp.float32)
            if kx == 1:
                for mem in products:
                    sums[mem][keep, :] = products[mem]
                step_done(l, mems, j, q)
                continue
            shift = DILATION_RATE if kx == 0 else m - DILATION_RATE
            moved = {
                mem: pltpu.roll(products[0 if shared else mem], shift if mem == 0 else m - shift, 0) for mem in mems
            }
            if kx == 0:
                before = {mem: sums[0 if shared else mem][keep, :] for mem in mems}
                for mem in mems:
                    sums[mem][keep, :] = before[mem] + moved[mem]
                step_done(l, mems, j, q)
                continue
            for mem in mems:
                conv = sums[mem][keep, :] + moved[mem]
                res = cur[0 if shared else mem][centre, :].astype(jnp.float32)
                y = residual_scale * (res + jnp.maximum(conv, 0.0))
                y = in_map_only(y.reshape(chunk, NC, C))
                if l < S - 1:
                    nxt[mem][centre, :] = y.reshape(m, C).astype(jnp.bfloat16)
                kept = stage if mem == 0 else stage2
                kept[l, pl.ds(place * chunk, chunk)] = y[:, halo : halo + CL, :].astype(jnp.bfloat16)

            if 0 in mems:
                @pl.when(sends(l))
                def _(l=l, q=q):
                    out_send(l, q).start()

                @pl.when(keeps(l))
                def _(l=l, q=q):
                    out_keep(l, q).start()

            if q == 1 and 1 in mems:
                if l < 2 and S > 2:
                    pl.when(my_pair > 0)(lambda: loss_of(l))
                else:
                    loss_of(l)
                if l == 2:
                    def earlier():
                        loss_of(0)
                        loss_of(1)
                    pl.when(my_pair == 0)(earlier)
            step_done(l, mems, j, q)

    own_sent(OWN, every[GO:])
    own_sent(DIRECT, every)

    @pl.when(low == 1)
    def _():
        own_sent(OWN, every[:GO])

    for k in range(1, pairs):
        for l in range(S):
            @pl.when(twin(k) == l)
            def _(k=k, l=l):
                for kx in ORDER:
                    for kind in routed(l):
                        forward(l, k, kx, kind).wait_send()
                    for kind in SHARES:
                        share(l, k, kx, kind).wait_send()
    for kx in ORDER:
        to_sib(kx).wait_send()

    for l in range(S):
        @pl.when(sends(l))
        def _(l=l):
            out_send(l, 0).wait_send()
            out_send(l, 1).wait_send()
            loss_send(l).wait_send()

        @pl.when(keeps(l))
        def _(l=l):
            out_keep(l, 0).wait()
            out_keep(l, 1).wait()
            loss_keep(l).wait()

    for b in range(M):
        sender = b + M * lax.rem(me, group)

        @pl.when(sender != me)
        def _(b=b, sender=sender):
            for h in range(2):
                half = R // 2
                place = pl.ds(pl.multiple_of((row if h == 0 else other_row) * half, half), half)
                dst = out_ref.at[b, place]
                remote(dst, dst, os_sem.at[0, h], or_sem.at[b, h], at(section=sender)).wait_recv()
            remote(loss_ref.at[b], loss_ref.at[b], ls_sem.at[0], lr_sem.at[b], at(section=sender)).wait_recv()


def finish(scale, out_ref, sums_ref, tissue_ref, result_ref, loss_ref, sem):
    move = pltpu.make_async_copy(out_ref, result_ref, sem)
    move.start()
    width = loss_ref.shape[-1]
    loss_ref[...] = tissue_ref[...].astype(jnp.float32) * (sums_ref[...][:, :, 0, :width] * scale)
    move.wait()


def local(features, conv_weight, tissue):
    S = lax.axis_size("section")
    n_col = lax.axis_size("col")
    M, R, CL, C = features.shape
    halo = DILATION_RATE * S
    NR, NC = R + halo, CL + 2 * halo
    pairs = S // 2
    rows_max = (NR - DILATION_RATE) * NC
    cfg = (S, M, R, CL, C, n_col, halo, NR, NC)
    anyspec = pl.BlockSpec(memory_space=pl.ANY)
    dma = pltpu.SemaphoreType.DMA
    act = pltpu.VMEM(((NR + 2 * DILATION_RATE) * NC, C), jnp.bfloat16)
    features = pltpu.with_memory_space_constraint(features, pltpu.HBM)
    kernels = pltpu.with_memory_space_constraint(conv_weight.reshape(TAPS, TAPS, C, C), pltpu.HBM)
    out, sums = pl.pallas_call(
        functools.partial(kernel, cfg),
        out_shape=(
            jax.ShapeDtypeStruct((M, R, CL, C), jnp.bfloat16),
            jax.ShapeDtypeStruct((M, R, 1, 128), jnp.float32),
        ),
        in_specs=[pl.BlockSpec(memory_space=pltpu.HBM)] * 2,
        out_specs=(anyspec, anyspec),
        scratch_shapes=[
            pltpu.VMEM((NR, CL, C), jnp.bfloat16),
            pltpu.VMEM((NR * halo, C), jnp.bfloat16),
            pltpu.VMEM((NR * halo, C), jnp.bfloat16),
            pltpu.VMEM((R * halo, C), jnp.bfloat16),
            pltpu.VMEM((R * halo, C), jnp.bfloat16),
            pltpu.VMEM((S, TAPS, TAPS, C, C), jnp.bfloat16),
            act, act, act, act,
            pltpu.VMEM((rows_max, C), jnp.float32),
            pltpu.VMEM((rows_max, C), jnp.float32),
            pltpu.VMEM((S, NR, CL, C), jnp.bfloat16),
            pltpu.VMEM((S, NR, CL, C), jnp.bfloat16),
            pltpu.VMEM((S, R, 1, 128), jnp.float32),
            dma((5,)), dma((5,)),
            dma((pairs, TAPS, 9)), dma((pairs, TAPS, 9)),
            dma((TAPS,)), dma((TAPS,)),
            pltpu.SemaphoreType.REGULAR,
            dma((S, 2)), dma((M, 2)),
            dma((S,)), dma((M,)),
            dma((7,)),
        ],
        compiler_params=pltpu.CompilerParams(
            collective_id=0, has_side_effects=True, vmem_limit_bytes=40 * 1024 * 1024
        ),
    )(features, kernels)
    result, loss = pl.pallas_call(
        functools.partial(finish, 1.0 / C),
        out_shape=(
            jax.ShapeDtypeStruct((M, R, CL, C), jnp.bfloat16),
            jax.ShapeDtypeStruct((M, R, CL), jnp.float32),
        ),
        in_specs=[anyspec, pl.BlockSpec(memory_space=pltpu.VMEM), pl.BlockSpec(memory_space=pltpu.VMEM)],
        out_specs=(pl.BlockSpec(memory_space=pltpu.HBM), pl.BlockSpec(memory_space=pltpu.VMEM)),
        scratch_shapes=[dma],
        compiler_params=pltpu.CompilerParams(vmem_limit_bytes=4 * 1024 * 1024),
    )(out, sums, tissue)
    return result[None], loss[None]


def solution(mesh):
    return jax.shard_map(
        local,
        mesh=mesh,
        in_specs=(
            P(None, "row", "col", None),
            P("section", None, None, None, None),
            P(None, "row", "col"),
        ),
        out_specs=(P("section", None, "row", "col", None), P("section", None, "row", "col")),
        check_vma=False,
    )
```

```python
import functools

import jax
import jax.numpy as jnp
from jax import lax
from jax.experimental import pallas as pl
from jax.experimental.pallas import tpu as pltpu
from jax.sharding import PartitionSpec as P

DILATION_RATE = 2
TAPS = 3
ORDER = (1, 0, 2)
residual_scale = 0.8
DIRECT_ROWS = (48, 64)
EARLY = 3
GO = 1
HOOKS = {
    (0, 2): (("gather", 2, 0), ("gather", 2, 1)),
    (1, 0): (("relay", 3, 0),),
    (1, 1): (("gather", 2, 2), ("relay", 3, 1)),
    (1, 2): (("relay", 3, 2),),
}
MESH = pl.DeviceIdType.MESH
OWN, DIRECT, ROW, COL, DIAG = range(5)


def kernel(cfg, f_ref, w_ref, out_ref, loss_ref, fwin, lstrip, rstrip, lpack, rpack, wall, a0, a1, b0, b1, s0, s1, stage, stage2, lstage,
           hs_sem, hr_sem, ws_sem, wr_sem, ks_sem, kr_sem, go_sem, os_sem, or_sem, ls_sem, lr_sem, loc_sem):
    S, M, R, CL, C, n_col, halo, NR, NC = cfg
    me = lax.axis_index("section")
    col = lax.axis_index("col")
    row = lax.axis_index("row")
    micro = lax.rem(me, M)
    group = S // M
    replica = me // M
    low = lax.rem(me, 2)
    sib = me + 1 - 2 * low
    pairs = S // 2
    my_pair = me // 2
    other_row = 1 - row
    mate = col + 1 - 2 * lax.rem(col, 2)
    has_left = col > 0
    has_right = col < n_col - 1
    quarter = C // 4
    directs = [rows * quarter // 64 for rows in DIRECT_ROWS]
    my_q = 2 * row + lax.rem(col, 2)

    def at(section=None, c=None, r=None):
        return {
            "section": me if section is None else section,
            "col": col if c is None else c,
            "row": row if r is None else r,
        }

    barrier = pltpu.get_barrier_semaphore()

    def hello(dev):
        pl.semaphore_signal(barrier, inc=1, device_id=dev, device_id_type=MESH)

    for d in range(1, S):
        hello(at(section=lax.rem(me + d, S)))
    hello(at(r=other_row))

    @pl.when(has_left)
    def _():
        hello(at(c=col - 1))
        hello(at(c=col - 1, r=other_row))

    @pl.when(has_right)
    def _():
        hello(at(c=col + 1))
        hello(at(c=col + 1, r=other_row))

    own_w = [pltpu.make_async_copy(w_ref.at[:, kx], wall.at[me, kx], loc_sem.at[kx]) for kx in range(TAPS)]
    own_f = pltpu.make_async_copy(
        f_ref.at[micro],
        fwin.at[pl.ds(row * halo, R)],
        loc_sem.at[3],
    )
    own_f.start()
    for kx in ORDER:
        own_w[kx].start()

    zeros = jnp.zeros((DILATION_RATE * NC, C), jnp.bfloat16)
    for ref in (a0, b0, b1, a1):
        ref[0 : DILATION_RATE * NC, :] = zeros
        ref[(DILATION_RATE + NR) * NC :, :] = zeros

    own_f.wait()
    edge = fwin[pl.ds(row * halo, R)].astype(jnp.float32)
    lpack[...] = edge[:, :halo, :].reshape(R * halo, C).astype(jnp.bfloat16)
    rpack[...] = edge[:, CL - halo :, :].reshape(R * halo, C).astype(jnp.bfloat16)

    greeted = 1 + (S - 1) + 2 * has_left.astype(jnp.int32) + 2 * has_right.astype(jnp.int32)
    pl.semaphore_wait(barrier, greeted)

    def remote(src, dst, s_sem, r_sem, dev):
        return pltpu.make_async_remote_copy(
            src_ref=src, dst_ref=dst, send_sem=s_sem, recv_sem=r_sem,
            device_id=dev, device_id_type=MESH,
        )

    def twin(k):
        a, b, res, bit = my_pair, k, 0, 1
        while bit < pairs:
            res = res + bit * lax.rem(a // bit + b // bit, 2)
            bit *= 2
        return 2 * res + low

    def rows_of(kind, direct=None):
        if kind == OWN:
            return my_q * quarter, quarter
        if kind == DIRECT:
            return (3 - my_q) * quarter, direct
        if kind == ROW:
            return (my_q + 2 - 4 * row) * quarter, quarter
        if kind == COL:
            return (my_q + 1 - 2 * lax.rem(col, 2)) * quarter, quarter
        if kind == DIAG:
            return (3 - my_q) * quarter + direct, quarter - direct

    def direct_of(l):
        return directs[l % 2]

    def routed(l):
        return (ROW, COL, DIAG) if direct_of(l) < quarter else (ROW, COL)

    def part(kind, direct):
        start, size = rows_of(kind, direct)
        return pl.ds(pl.multiple_of(start, 16), size)

    def sent_part(kind, direct):
        if kind == DIAG:
            return pl.ds(pl.multiple_of(my_q * quarter + direct, 16), quarter - direct)
        return part(OWN, direct)

    def give(k, kx, kind, direct):
        piece = part(kind, direct)
        return remote(w_ref.at[:, kx, piece], wall.at[me, kx, :, piece],
                      ws_sem.at[k, kx, kind], wr_sem.at[k, kx, kind], at(section=twin(k)))

    def forward(l, k, kx, kind):
        piece = sent_part(kind, direct_of(l))
        dev = {ROW: at(r=other_row), COL: at(c=mate), DIAG: at(c=mate, r=other_row)}[kind]
        slot = wall.at[l, kx, :, piece]
        return remote(slot, slot, ws_sem.at[k, kx, kind], wr_sem.at[k, kx, kind], dev)

    def arrival(l, k, kx, kind):
        slot = wall.at[l, kx, :, part(kind, direct_of(l))]
        return remote(slot, slot, ws_sem.at[k, kx, kind], wr_sem.at[k, kx, kind], at(section=twin(k)))

    SHARES = (OWN, ROW, COL, DIAG)

    def share(l, k, kx, kind):
        start = rows_of(DIRECT, directs[0])[0] if kind == DIAG else rows_of(kind)[0]
        slot = wall.at[l, kx, :, pl.ds(pl.multiple_of(start, 16), quarter)]
        n = 5 + SHARES.index(kind)
        return remote(slot, slot, ws_sem.at[k, kx, n], wr_sem.at[k, kx, n], at(section=sib))

    def to_sib(kx):
        return remote(w_ref.at[:, kx], wall.at[me, kx], ks_sem.at[kx], kr_sem.at[kx], at(section=sib))

    def send_own(kind, js):
        for first, direct in enumerate(directs):
            @pl.when(low == first)
            def _(direct=direct):
                for j in js:
                    for k in range(1, pairs):
                        give(k, ORDER[j], kind, direct).start()

    def own_sent(kind, js):
        for first, direct in enumerate(directs):
            @pl.when(low == first)
            def _(direct=direct):
                for j in js:
                    for k in range(1, pairs):
                        give(k, ORDER[j], kind, direct).wait_send()

    def relay(l, kx):
        for k in range(1, pairs):
            @pl.when(twin(k) == l)
            def _(k=k):
                arrival(l, k, kx, OWN).wait_recv()
                for kind in routed(l):
                    forward(l, k, kx, kind).start()
                share(l, k, kx, OWN).start()

    def gather(l, kx):
        for k in range(1, pairs):
            @pl.when(twin(k) == l)
            def _(k=k):
                for kind in (COL, ROW):
                    arrival(l, k, kx, kind).wait_recv()
                    share(l, k, kx, kind).start()
                arrival(l, k, kx, DIRECT).wait_recv()
                if DIAG in routed(l):
                    arrival(l, k, kx, DIAG).wait_recv()
                share(l, k, kx, DIAG).start()

    def complete(l, kx, gathered):
        @pl.when(me == l)
        def _():
            own_w[kx].wait()

        @pl.when(sib == l)
        def _():
            to_sib(kx).wait_recv()

        if gathered is None:
            gather(l, kx)
        elif gathered is not True:
            pl.when(jnp.logical_not(gathered))(lambda: gather(l, kx))
        for k in range(1, pairs):
            @pl.when(twin(k) + 1 - 2 * low == l)
            def _(k=k):
                for kind in SHARES:
                    share(l, k, kx, kind).wait_recv()

    every = range(TAPS)

    @pl.when(low == 0)
    def _():
        send_own(OWN, every)
        send_own(DIRECT, every[:EARLY])


    def strip(start, count):
        return pl.ds(pl.multiple_of(start * halo, 16), count * halo)

    out_row, in_row = (1 - row) * (R - halo), row * R
    here, across, into = strip(row * halo, R), strip(out_row, halo), strip(in_row, halo)
    to_left = remote(lpack, rstrip.at[here], hs_sem.at[0], hr_sem.at[0], at(c=col - 1))
    to_right = remote(rpack, lstrip.at[here], hs_sem.at[1], hr_sem.at[1], at(c=col + 1))
    to_row = remote(f_ref.at[micro, pl.ds(out_row, halo)], fwin.at[pl.ds(in_row, halo)], hs_sem.at[2], hr_sem.at[2], at(r=other_row))
    to_dl = remote(lpack.at[across], rstrip.at[into], hs_sem.at[3], hr_sem.at[3], at(c=col - 1, r=other_row))
    to_dr = remote(rpack.at[across], lstrip.at[into], hs_sem.at[4], hr_sem.at[4], at(c=col + 1, r=other_row))
    to_row.start()

    @pl.when(has_left)
    def _():
        to_left.start()
        to_dl.start()

    @pl.when(has_right)
    def _():
        to_right.start()
        to_dr.start()

    for kx in ORDER:
        to_sib(kx).start()

    def first_even(j):
        kx = ORDER[j]
        relay(0, kx)
        if pairs > 1:
            pl.when(my_pair == 0)(lambda: relay(2, kx))

    @pl.when(low == 0)
    def _():
        own_sent(OWN, every[:GO])
        pl.semaphore_signal(go_sem, inc=1, device_id=at(section=sib), device_id_type=MESH)

    @pl.when(low == 1)
    def _():
        pl.semaphore_wait(go_sem, 1)
        send_own(OWN, every)
        send_own(DIRECT, every)

    first_even(0)
    first_even(1)

    def in_map_only(v):
        return jnp.concatenate(
            [
                jnp.where(has_left, v[:, :halo], 0.0),
                v[:, halo : halo + CL],
                jnp.where(has_right, v[:, halo + CL :], 0.0),
            ],
            axis=1,
        )

    def fill(start, count):
        for i in range(0, count, 4):
            at_row = start + i
            side = strip(at_row, 4)
            v = jnp.concatenate(
                [
                    jnp.where(has_left, lstrip[side, :].astype(jnp.float32).reshape(4, halo, C), 0.0),
                    fwin[pl.ds(at_row, 4)].astype(jnp.float32),
                    jnp.where(has_right, rstrip[side, :].astype(jnp.float32).reshape(4, halo, C), 0.0),
                ],
                axis=1,
            )
            place = pl.ds(pl.multiple_of((at_row + DILATION_RATE) * NC, 16), 4 * NC)
            a0[place, :] = v.reshape(4 * NC, C).astype(jnp.bfloat16)

    def sides_in():
        @pl.when(has_left)
        def _():
            to_left.wait_send()
            to_right.wait_recv()

        @pl.when(has_right)
        def _():
            to_right.wait_send()
            to_left.wait_recv()

        fill(row * halo, R)

    def rows_come_in():
        to_row.wait()

        @pl.when(has_left)
        def _():
            to_dl.wait_send()
            to_dr.wait_recv()

        @pl.when(has_right)
        def _():
            to_dr.wait_send()
            to_dl.wait_recv()

        fill((1 - row) * R, halo)

    sides_in()
    first_even(2)
    pl.when(low == 0)(lambda: send_own(DIRECT, every[EARLY:]))
    split_first = halo + DILATION_RATE <= R
    if not split_first:
        rows_come_in()

    def after(l, j):
        if pairs > 1:
            if (l, j) in HOOKS:
                def meanwhile():
                    for what, t, i in HOOKS[(l, j)]:
                        (gather if what == "gather" else relay)(t, ORDER[i])
                pl.when(my_pair == 0)(meanwhile)
        if j == 2 and l + 2 < S and l + 2 >= 2:
            t = l + 2
            for kk in ORDER:
                if t in (2, 3):
                    pl.when(my_pair > 0)(lambda t=t, kk=kk: relay(t, kk))
                else:
                    relay(t, kk)

    def step_done(l, mems, j, q):
        if l == 0 and q == 0:
            pl.when(my_pair > 0)(lambda: relay(1, ORDER[j]))
        if q == 1 and len(mems) == 2:
            after(l, j)
        elif (q, j) == (1, 2) and mems == (0,):
            after(l, 0)
            after(l, 1)
        elif (q, j) == (1, 2):
            after(l, 2)

    def out_copy(l, h):
        n = NR - DILATION_RATE * (l + 1)
        half = R // 2
        place = pl.ds(pl.multiple_of((row if h == 0 else other_row) * half, half), half)
        src = stage.at[l, pl.ds(row * (n - R) + (row if h == 0 else other_row) * half, half)]
        return src, out_ref.at[micro, place]

    def loss_copy(l):
        return lstage.at[l], loss_ref.at[micro]

    def out_send(l, h):
        src, dst = out_copy(l, h)
        return remote(src, dst, os_sem.at[l, h], or_sem.at[micro, h], at(section=l))

    def loss_send(l):
        src, dst = loss_copy(l)
        return remote(src, dst, ls_sem.at[l], lr_sem.at[micro], at(section=l))

    def out_keep(l, h):
        src, dst = out_copy(l, h)
        return pltpu.make_async_copy(src, dst, loc_sem.at[4 + h])

    def loss_keep(l):
        src, dst = loss_copy(l)
        return pltpu.make_async_copy(src, dst, loc_sem.at[6])

    def sends(l):
        return jnp.logical_and(replica == l % group, me != l)

    def keeps(l):
        return jnp.logical_and(replica == l % group, me == l)

    def loss_of(l):
        n = NR - DILATION_RATE * (l + 1)
        own = pl.ds(row * (n - R), R)
        d = stage[l, own].astype(jnp.float32) - stage2[l, own].astype(jnp.float32)
        d = jnp.sum(d * d, axis=-1, keepdims=True)
        lstage[l] = jnp.sum(jnp.where(eye, d, 0.0), axis=1, keepdims=True)
        pl.when(sends(l))(lambda: loss_send(l).start())
        pl.when(keeps(l))(lambda: loss_keep(l).start())

    eye = lax.broadcasted_iota(jnp.int32, (1, CL, 128), 1) == lax.broadcasted_iota(jnp.int32, (1, CL, 128), 2)

    for l in range(S):
        n = NR - DILATION_RATE * (l + 1)
        r0 = row * (NR - n)
        chunk = n // 2
        m = chunk * NC
        cur, nxt = ((a0, a1), (b0, b1))[l % 2], ((a0, a1), (b0, b1))[(l + 1) % 2]
        sums = (s0, s1)
        shared = l == 0
        both = (0, 1)
        if shared:
            steps = [(both, j, q) for q in range(2) for j in range(TAPS)]
        elif l < 2:
            steps = [(both, j, q) for j in range(TAPS) for q in range(2)]
        else:
            steps = [((mem,), j, q) for mem in both for j in range(TAPS) for q in range(2)]
        for mems, j, q in steps:
            kx = ORDER[j]
            if q == 0 and 0 in mems:
                complete(l, kx, (my_pair == 0) if l == 2 else None)
            if shared and split_first and (j, q) == (0, 1):
                rows_come_in()
            w = wall[l, kx].reshape(TAPS * C, C)
            place = row if q == 0 else other_row
            base = r0 + place * chunk
            keep = pl.ds(q * m, m)
            centre = pl.ds(pl.multiple_of((base + DILATION_RATE) * NC, 16), m)
            products = {}
            for mem in (0,) if shared else mems:
                lhs = jnp.concatenate(
                    [cur[mem][pl.ds(pl.multiple_of((base + DILATION_RATE * ky) * NC, 16), m), :] for ky in range(TAPS)],
                    axis=1,
                )
                products[mem] = jnp.dot(lhs, w, preferred_element_type=jnp.float32)
            if kx == 1:
                for mem in products:
                    sums[mem][keep, :] = products[mem]
                step_done(l, mems, j, q)
                continue
            shift = DILATION_RATE if kx == 0 else m - DILATION_RATE
            moved = {
                mem: pltpu.roll(products[0 if shared else mem], shift if mem == 0 else m - shift, 0) for mem in mems
            }
            if kx == 0:
                before = {mem: sums[0 if shared else mem][keep, :] for mem in mems}
                for mem in mems:
                    sums[mem][keep, :] = before[mem] + moved[mem]
                step_done(l, mems, j, q)
                continue
            for mem in mems:
                conv = sums[mem][keep, :] + moved[mem]
                res = cur[0 if shared else mem][centre, :].astype(jnp.float32)
                y = residual_scale * (res + jnp.maximum(conv, 0.0))
                y = in_map_only(y.reshape(chunk, NC, C))
                if l < S - 1:
                    nxt[mem][centre, :] = y.reshape(m, C).astype(jnp.bfloat16)
                kept = stage if mem == 0 else stage2
                kept[l, pl.ds(place * chunk, chunk)] = y[:, halo : halo + CL, :].astype(jnp.bfloat16)

            if 0 in mems:
                @pl.when(sends(l))
                def _(l=l, q=q):
                    out_send(l, q).start()

                @pl.when(keeps(l))
                def _(l=l, q=q):
                    out_keep(l, q).start()

            if q == 1 and 1 in mems:
                if l < 2 and S > 2:
                    pl.when(my_pair > 0)(lambda: loss_of(l))
                else:
                    loss_of(l)
                if l == 2:
                    def earlier():
                        loss_of(0)
                        loss_of(1)
                    pl.when(my_pair == 0)(earlier)
            step_done(l, mems, j, q)

    own_sent(OWN, every[GO:])
    own_sent(DIRECT, every)

    @pl.when(low == 1)
    def _():
        own_sent(OWN, every[:GO])

    for k in range(1, pairs):
        for l in range(S):
            @pl.when(twin(k) == l)
            def _(k=k, l=l):
                for kx in ORDER:
                    for kind in routed(l):
                        forward(l, k, kx, kind).wait_send()
                    for kind in SHARES:
                        share(l, k, kx, kind).wait_send()
    for kx in ORDER:
        to_sib(kx).wait_send()

    for l in range(S):
        @pl.when(sends(l))
        def _(l=l):
            out_send(l, 0).wait_send()
            out_send(l, 1).wait_send()
            loss_send(l).wait_send()

        @pl.when(keeps(l))
        def _(l=l):
            out_keep(l, 0).wait()
            out_keep(l, 1).wait()
            loss_keep(l).wait()

    for b in range(M):
        sender = b + M * lax.rem(me, group)

        @pl.when(sender != me)
        def _(b=b, sender=sender):
            for h in range(2):
                half = R // 2
                place = pl.ds(pl.multiple_of((row if h == 0 else other_row) * half, half), half)
                dst = out_ref.at[b, place]
                remote(dst, dst, os_sem.at[0, h], or_sem.at[b, h], at(section=sender)).wait_recv()
            remote(loss_ref.at[b], loss_ref.at[b], ls_sem.at[0], lr_sem.at[b], at(section=sender)).wait_recv()


def finish(scale, out_ref, sums_ref, tissue_ref, result_ref, loss_ref, sem):
    move = pltpu.make_async_copy(out_ref, result_ref, sem)
    move.start()
    width = loss_ref.shape[-1]
    loss_ref[...] = tissue_ref[...].astype(jnp.float32) * (sums_ref[...][:, :, 0, :width] * scale)
    move.wait()


def local(features, conv_weight, tissue):
    S = lax.axis_size("section")
    n_col = lax.axis_size("col")
    M, R, CL, C = features.shape
    halo = DILATION_RATE * S
    NR, NC = R + halo, CL + 2 * halo
    pairs = S // 2
    rows_max = (NR - DILATION_RATE) * NC
    cfg = (S, M, R, CL, C, n_col, halo, NR, NC)
    anyspec = pl.BlockSpec(memory_space=pl.ANY)
    dma = pltpu.SemaphoreType.DMA
    act = pltpu.VMEM(((NR + 2 * DILATION_RATE) * NC, C), jnp.bfloat16)
    features = pltpu.with_memory_space_constraint(features, pltpu.HBM)
    kernels = pltpu.with_memory_space_constraint(conv_weight.reshape(TAPS, TAPS, C, C), pltpu.HBM)
    out, sums = pl.pallas_call(
        functools.partial(kernel, cfg),
        out_shape=(
            jax.ShapeDtypeStruct((M, R, CL, C), jnp.bfloat16),
            jax.ShapeDtypeStruct((M, R, 1, 128), jnp.float32),
        ),
        in_specs=[pl.BlockSpec(memory_space=pltpu.HBM)] * 2,
        out_specs=(anyspec, anyspec),
        scratch_shapes=[
            pltpu.VMEM((NR, CL, C), jnp.bfloat16),
            pltpu.VMEM((NR * halo, C), jnp.bfloat16),
            pltpu.VMEM((NR * halo, C), jnp.bfloat16),
            pltpu.VMEM((R * halo, C), jnp.bfloat16),
            pltpu.VMEM((R * halo, C), jnp.bfloat16),
            pltpu.VMEM((S, TAPS, TAPS, C, C), jnp.bfloat16),
            act, act, act, act,
            pltpu.VMEM((rows_max, C), jnp.float32),
            pltpu.VMEM((rows_max, C), jnp.float32),
            pltpu.VMEM((S, NR, CL, C), jnp.bfloat16),
            pltpu.VMEM((S, NR, CL, C), jnp.bfloat16),
            pltpu.VMEM((S, R, 1, 128), jnp.float32),
            dma((5,)), dma((5,)),
            dma((pairs, TAPS, 9)), dma((pairs, TAPS, 9)),
            dma((TAPS,)), dma((TAPS,)),
            pltpu.SemaphoreType.REGULAR,
            dma((S, 2)), dma((M, 2)),
            dma((S,)), dma((M,)),
            dma((7,)),
        ],
        compiler_params=pltpu.CompilerParams(
            collective_id=0, has_side_effects=True, vmem_limit_bytes=40 * 1024 * 1024
        ),
    )(features, kernels)
    result, loss = pl.pallas_call(
        functools.partial(finish, 1.0 / C),
        out_shape=(
            jax.ShapeDtypeStruct((M, R, CL, C), jnp.bfloat16),
            jax.ShapeDtypeStruct((M, R, CL), jnp.float32),
        ),
        in_specs=[anyspec, pl.BlockSpec(memory_space=pltpu.VMEM), pl.BlockSpec(memory_space=pltpu.VMEM)],
        out_specs=(pl.BlockSpec(memory_space=pltpu.HBM), pl.BlockSpec(memory_space=pltpu.VMEM)),
        scratch_shapes=[dma],
        compiler_params=pltpu.CompilerParams(vmem_limit_bytes=4 * 1024 * 1024),
    )(out, sums, tissue)
    return result[None], loss[None]


def solution(mesh):
    return jax.shard_map(
        local,
        mesh=mesh,
        in_specs=(
            P(None, "row", "col", None),
            P("section", None, None, None, None),
            P(None, "row", "col"),
        ),
        out_specs=(P("section", None, "row", "col", None), P("section", None, "row", "col")),
        check_vma=False,
    )
```
